32 devices in a mesh: section: 8 (over y, x, core), tensor: 4 (over z).
Axes of the slice: x: 2, y: 2, z: 4, core: 2. Of those that a mesh axis runs over, the one named last changes fastest.
Arguments:
- states: bfloat16 [4096, 8192], P('section', 'tensor'), may hold values from -6 to 6
- lengths: int32 [8, 16], P('section'), may hold values from 1 to 96, 512 in all within a row
- routes: int32 [4096, 1], P('section'), may hold values from 0 to 7; in each aligned block of 512 rows (0 to 511, 512 to 1023, ...) at most 128 rows name the same one
- score_gain: float32 [8, 8192], P('section'), may hold values from 0.25 to 1.75
- score_weight: bfloat16 [8, 8192, 4096], P('section', None, 'tensor'), may hold values from -0.0625 to 0.0625
- score_heads: float32 [8, 4096, 2], P('section', 'tensor'), may hold values from -0.09375 to 0.09375
- actor_gain: float32 [8192], replicated, may hold values from 0.25 to 1.75
- actor_weight: bfloat16 [8192, 4096], P(None, 'tensor'), may hold values from -0.0625 to 0.0625
- actor_heads: float32 [4096], P('tensor'), may hold values from -0.09375 to 0.09375
Outputs:
- packed_scores: float32 [2, 8192], P(None, 'section')
- advantages: float32 [4096], P('section')
- actor_grad: float32 [8192, 4096], P('section', 'tensor')
The draws below stay inside these ranges and needn't reach their ends.
Inputs may be any that keep to these rules, and one draw needn't show every extreme that they name: `lengths`: each row sums to 512; its largest entry is exactly 96. `routes`: in the rows of one section (aligned blocks of 512 rows) no member is named by more than 128 rows; some member is named by exactly 128 rows of some block.
All inputs are finite; a program needn't handle non-finite values.
Results may differ from the reference program's by a relative error of at most 0.0055.
Values may be sent and summed in bfloat16 or wider, within the bound.
A program may use at most 128 MiB of HBM per device.

```python
import math
import jax
import jax.numpy as jnp
import numpy as np
from jax import lax

D = 8192
HID = 4096
TOK_SEC = 512
RESP_SEC = 16
LEN_MAX = 96
CAP = 128
SLOTS = 1024
TOKENS = 4096
N_SECTION = 8


def level_of(key, extent, shards, low, top_value):
    gain = 1.0
    for dim, parts in shards:
        steps = jax.random.uniform(jax.random.fold_in(jax.random.fold_in(key, 6), dim), (parts,), jnp.float32, low / len(shards), top_value / len(shards))
        gain = gain * jnp.repeat(jnp.exp(steps), extent[dim] // parts).reshape((-1,) + (1,) * (len(extent) - 1 - dim))
    return gain


def split_up(amount, total, bound, lean):
    loads = [(1 << 20) // math.isqrt(standing ** lean) + 1 for standing in range(2, amount + 1)]
    rest, holding = total - bound - (amount - 1), [1] * (amount - 1)
    while rest > 0:
        candidates = [i for i in range(amount - 1) if holding[i] < bound]
        mass, budget = sum([loads[i] for i in candidates]), rest
        for i in candidates:
            extra = min(bound - holding[i], max(1, budget * loads[i] // mass), rest)
            holding[i] = holding[i] + extra
            rest = rest - extra
    return np.array([bound] + holding)


def uneven(stream_key, count, total, limit, skew):
    if count == 2:
        one = jax.random.randint(stream_key, (), max(1, total - limit), min(limit, total - 1) + 1)
        return jnp.stack([one, total - one])
    tallies = jnp.asarray(split_up(count, total, limit, skew), jnp.int32)
    couples = (count - 1) // 2
    giver, receiver = tallies[1:1 + 2 * couples:2], tallies[2:2 + 2 * couples:2]
    margin = jnp.minimum(giver - 1, limit - receiver)
    passed = jax.random.randint(jax.random.fold_in(stream_key, 1), (couples,), 0, 1 << 20) % (margin + 1)
    tallies = tallies.at[1:1 + 2 * couples:2].set(giver - passed).at[2:2 + 2 * couples:2].set(receiver + passed)
    return tallies[jax.random.permutation(jax.random.fold_in(stream_key, 2), count)]


def shared_out(stream_key, own, number, rows, count, top, limit, lean):
    order = jax.random.permutation(stream_key, count)
    crowded, common = shares(count, rows * top, limit, lean, True), shares(count, rows * top, limit, lean, False)
    places = jnp.arange(count)

    def named(sizes, rotation):
        used = int((sizes > 0).sum())
        fixed = max(1, used // 4)
        shifted = fixed + (places - fixed + rotation * (used - fixed)) % max(1, count - fixed)
        return jnp.zeros((count,), jnp.int32).at[order[jnp.where(places < fixed, places, shifted)]].set(jnp.asarray(sizes, jnp.int32))

    sizes = jnp.where(number % 4 == 0, named(crowded, number // 4), named(common, number - number // 4 - 1))
    mixed = jax.random.permutation(jax.random.fold_in(own, 3), count)
    giver, receiver = mixed[0:count // 2 * 2:2], mixed[1:count // 2 * 2:2]
    margin = jnp.minimum(sizes[giver] - 1, limit - sizes[receiver]) // 2
    margin = jnp.where((giver == order[0]) | (receiver == order[0]) | (sizes[receiver] == 0), 0, jnp.maximum(margin, 0))
    shifted = jax.random.randint(jax.random.fold_in(own, 4), (count // 2,), 0, 1 << 20) % (margin + 1)
    sizes = sizes.at[giver].add(-shifted).at[receiver].add(shifted)
    labels = jnp.searchsorted(jnp.cumsum(sizes), jnp.arange(rows * top), side="right").astype(jnp.int32)
    grid = labels.reshape(top, rows).T
    grid = grid[jax.random.permutation(jax.random.fold_in(own, 1), rows)]
    rotation = jax.random.randint(jax.random.fold_in(own, 2), (rows, 1), 0, top)
    return jnp.take_along_axis(grid, (jnp.arange(top)[None, :] + rotation) % top, axis=1)


def shares(count, total, limit, slope, full):
    loads = [(1 << 20) // math.isqrt(standing ** slope) + 1 for standing in range(1, count + 1)]
    largest = limit if full else min(limit, max(-(-total // count), total * loads[0] // sum(loads)))
    least = 1 if total - largest >= count - 1 else 0
    counts, spare = [largest] + [least] * (count - 1), total - largest - least * (count - 1)
    while spare > 0:
        candidates = [i for i in range(1, count) if counts[i] < largest] or [i for i in range(1, count) if counts[i] < limit]
        mass, budget = sum([loads[i] for i in candidates]), spare
        for i in candidates:
            extra = min(limit - counts[i], max(1, budget * loads[i] // mass), spare)
            counts[i] = counts[i] + extra
            spare = spare - extra
    return np.array(counts)


def normal_values(rng, shape, scale, limit, pieces=(), held_as=jnp.bfloat16):
    array = scale * jax.random.normal(rng, shape, jnp.float32)
    if pieces:
        array = array * level_of(rng, shape, pieces, -0.22, 0.18)
    return jnp.clip(array, -limit, limit).astype(held_as)


def setup_inputs(seed: int = 0) -> dict:
    splits = jax.random.split(jax.random.key(seed), 10)
    states = normal_values(splits[0], (TOKENS, D), 1.0, 6.0, ((0, 8), (1, 4)))
    lengths = jax.vmap(lambda own: uneven(own, RESP_SEC, TOK_SEC, LEN_MAX, 2))(jax.random.split(splits[1], N_SECTION)).reshape((N_SECTION, RESP_SEC)).astype(jnp.int32)
    routes_keys = jax.random.split(jax.random.fold_in(splits[2], 1), TOKENS // TOK_SEC)
    routes_turns = jax.random.permutation(jax.random.fold_in(splits[2], 3), TOKENS // TOK_SEC)
    routes = jax.vmap(lambda own, number: shared_out(jax.random.fold_in(splits[2], 2), own, number, TOK_SEC, N_SECTION, 1, CAP, 2))(routes_keys, routes_turns).reshape((TOKENS, 1))
    score_gain = jnp.clip(1.0 + 0.15 * jax.random.normal(splits[3], (N_SECTION, D), jnp.float32), 0.25, 1.75)
    score_weight = normal_values(splits[4], (N_SECTION, D, HID), D ** -0.5, 0.0625, ((0, 8), (2, 4)))
    score_heads = normal_values(splits[5], (N_SECTION, HID, 2), HID ** -0.5, 0.09375, ((0, 8), (1, 4)), jnp.float32)
    actor_gain = jnp.clip(1.0 + 0.15 * jax.random.normal(splits[6], (D,), jnp.float32), 0.25, 1.75)
    actor_weight = normal_values(splits[7], (D, HID), D ** -0.5, 0.0625, ((1, 4),))
    actor_heads = normal_values(splits[8], (HID,), HID ** -0.5, 0.09375, ((0, 4),), jnp.float32)
    return {"states": states, "lengths": lengths, "routes": routes, "score_gain": score_gain, "score_weight": score_weight, "score_heads": score_heads, "actor_gain": actor_gain, "actor_weight": actor_weight, "actor_heads": actor_heads}


epsilon = 1e-05
trace_decay = 0.95
penalty = 0.1

def compose(earlier, later):
    return (earlier[0] * later[0], later[1] + later[0] * earlier[1])

def advantage_rows(values, rewards, lengths):
    ends = jnp.cumsum(lengths, axis=1) - 1
    steps_idx = jnp.arange(values.shape[1], dtype=jnp.int32)
    last = jnp.any(steps_idx[None, :, None] == ends[:, None, :], axis=2)
    following = jnp.concatenate([values[:, 1:], jnp.zeros_like(values[:, :1])], axis=1)
    delta = jnp.where(last, rewards, following) - values
    weight = jnp.where(last, 0.0, trace_decay).astype(values.dtype)
    carried = lax.associative_scan(compose, (weight[:, ::-1], delta[:, ::-1]), axis=1)
    return carried[1][:, ::-1]

def reference(states, lengths, routes, score_gain, score_weight, score_heads, actor_gain, actor_weight, actor_heads):
    target = routes[:, 0].astype(jnp.int32)
    source = (jnp.arange(TOKENS, dtype=jnp.int32) // TOK_SEC).astype(jnp.int32)
    onehot = (target[:, None] == jnp.arange(N_SECTION, dtype=jnp.int32)[None, :]).astype(jnp.int32)
    blocked = onehot.reshape(N_SECTION, TOK_SEC, N_SECTION)
    before = (jnp.cumsum(blocked, axis=1) - blocked).reshape(TOKENS, N_SECTION)
    placed = lax.optimization_barrier(jnp.sum(before * onehot, axis=1)).astype(jnp.int32)
    slot_index = (source * CAP + placed).astype(jnp.int32)
    packed = jnp.zeros((N_SECTION, SLOTS, D), jnp.bfloat16).at[target, slot_index].set(states)

    def member(member_args):
        row_block, gain_row, member_weight, head_cols = member_args
        widened = row_block.astype(jnp.float32)
        member_scale = lax.rsqrt(lax.optimization_barrier(jnp.mean(widened * widened, axis=1)) + epsilon)
        scaled = (widened * gain_row[None, :]).astype(jnp.bfloat16)
        preact = jnp.dot(scaled, member_weight, preferred_element_type=jnp.float32) * member_scale[:, None]
        return jnp.dot(jax.nn.silu(preact), head_cols, precision=lax.Precision.HIGHEST)
    scored = lax.map(member, (packed, score_gain, score_weight, score_heads))
    packed_scores = jnp.transpose(scored, (2, 0, 1)).reshape(2, N_SECTION * SLOTS)
    token_scores = scored[target, slot_index]
    values = token_scores[:, 0].reshape(N_SECTION, TOK_SEC)
    rewards = token_scores[:, 1].reshape(N_SECTION, TOK_SEC)
    raw_adv = advantage_rows(values, rewards, lengths)
    center = jnp.sum(raw_adv) / TOKENS
    spread = jnp.sum(raw_adv * raw_adv) / TOKENS - center * center
    advantages = ((raw_adv - center) * lax.rsqrt(spread + epsilon)).reshape(TOKENS)
    widened = states.astype(jnp.float32)
    actor_scale = lax.rsqrt(lax.optimization_barrier(jnp.mean(widened * widened, axis=1)) + epsilon)
    gained = (widened * actor_gain[None, :]).astype(jnp.bfloat16)
    actor_pre = jnp.dot(gained, actor_weight, preferred_element_type=jnp.float32) * actor_scale[:, None]
    log_shift = jnp.dot(jax.nn.silu(actor_pre), actor_heads, precision=lax.Precision.HIGHEST)
    ratios = jnp.exp(log_shift)
    logit_slope = penalty * (ratios - 1.0) - ratios * advantages
    sigmoid_pre = jax.nn.sigmoid(actor_pre)
    silu_slope = sigmoid_pre * (1.0 + actor_pre * (1.0 - sigmoid_pre))
    grad_pre = ((logit_slope * actor_scale)[:, None] * actor_heads[None, :] * silu_slope).astype(jnp.bfloat16)
    actor_grad = jnp.dot(gained.T, grad_pre, preferred_element_type=jnp.float32)
    return (packed_scores, advantages, actor_grad)
```

```python
import functools
import jax
import jax.numpy as jnp
from jax import lax
from jax.experimental import pallas as pl
from jax.experimental.pallas import tpu as pltpu
from jax.sharding import PartitionSpec as P

epsilon = 1e-05
trace_decay = 0.95
penalty = 0.1
MESH = pl.DeviceIdType.MESH


def exchange(
    sections, tensors, cap, reach,
    states, routes, lengths, gain_m, gain_a, weight_m, weight_a, heads_m, heads_a,
    scores, pairs, blocks, hidden,
    acc_m, acc_a, sq_m, sq_a, lanes, part, part_a, back, early, feats, outbox, inbox, work, wbuf_m, wbuf_a,
    dispatch, ended,
    z_send, z_recv, m_send, m_recv, l_send, l_recv, b_send, b_recv, loc_sem, w_sem,
    t_send, t_recv, u_send, u_recv, r_send, r_recv, p_send, p_recv, g_send, g_recv, g_pass,
    h_send, h_recv, q_send, q_recv, y_send, y_recv,
):
    s = lax.axis_index("section")
    t = lax.axis_index("tensor")
    tok, fs = states.shape
    slots = sections * cap
    bps = sections // tensors
    bw = fs // bps
    hid = acc_m.shape[1]
    nt = min(hid, 256)
    chunks = 2
    half = tok // chunks
    up_ok = t + 1 < tensors
    dn_ok = t > 0
    chips = sections // 2
    chip = s // 2
    core = lax.rem(s, 2)
    partner = s + 1 - 2 * core
    far = chips - 1 - chip
    near = slots - 2 * cap
    share = tok // tensors
    width = fs * tensors
    rb = 64

    def place(src, dest):
        return lax.rem(src // 2 + dest // 2, chips) * 2 + lax.rem(src, 2)

    load = pltpu.make_async_copy(states, feats.at[t], loc_sem.at[0])
    load.start()

    barrier = pltpu.get_barrier_semaphore()

    def greet(r, c):
        pl.semaphore_signal(barrier, inc=1, device_id=(lax.rem(s + r, sections), t), device_id_type=MESH)
        return c

    lax.fori_loop(1, sections, greet, 0)

    def greet_z(r, c):
        pl.semaphore_signal(barrier, inc=1, device_id=(s, lax.rem(t + r, tensors)), device_id_type=MESH)
        return c

    lax.fori_loop(1, tensors, greet_z, 0)
    pl.semaphore_wait(barrier, sections - 1 + tensors - 1)
    load.wait()

    def z_copy(way, hop, c, shard, dest):
        rows = pl.ds(c * half, half)
        return pltpu.make_async_remote_copy(
            src_ref=feats.at[shard, rows], dst_ref=feats.at[shard, rows],
            send_sem=z_send.at[way, hop, c], recv_sem=z_recv.at[way, hop, c],
            device_id=(s, dest), device_id_type=MESH,
        )

    def m_copy(k, dest, src):
        return pltpu.make_async_remote_copy(
            src_ref=outbox.at[k, pl.ds(pl.multiple_of(dest * cap, cap), cap)],
            dst_ref=inbox.at[k, pl.ds(pl.multiple_of(place(src, dest) * cap, cap), cap)],
            send_sem=m_send.at[k, dest], recv_sem=m_recv.at[k, src],
            device_id=(dest, t), device_id_type=MESH,
        )

    def own_copy(k):
        return pltpu.make_async_copy(
            outbox.at[k, pl.ds(pl.multiple_of(s * cap, cap), cap)],
            inbox.at[k, pl.ds(pl.multiple_of(place(s, s) * cap, cap), cap)],
            m_recv.at[k, s],
        )

    def l_copy(way, hop, k, dest):
        rows = pl.ds(near, 2 * cap)
        return pltpu.make_async_remote_copy(
            src_ref=inbox.at[k, rows], dst_ref=inbox.at[k, rows],
            send_sem=l_send.at[way, hop], recv_sem=l_recv.at[way, hop],
            device_id=(s, dest), device_id_type=MESH,
        )

    def b_src(dest, row, count):
        return feats.at[dest // bps, pl.ds(row, count), pl.ds(pl.multiple_of(lax.rem(dest, bps) * bw, bw), bw)]

    def b_copy(dest, src):
        return pltpu.make_async_remote_copy(
            src_ref=b_src(dest, 0, tok), dst_ref=blocks.at[src],
            send_sem=b_send.at[dest], recv_sem=b_recv.at[src],
            device_id=(dest, t), device_id_type=MESH,
        )

    def own_block():
        return pltpu.make_async_copy(b_src(s, 0, tok), blocks.at[s], b_recv.at[s])

    def q_copy(dest, src):
        row = pl.multiple_of(t * share, 16)
        return pltpu.make_async_remote_copy(
            src_ref=b_src(dest, row, share), dst_ref=blocks.at[src, pl.ds(row, share)],
            send_sem=q_send.at[dest], recv_sem=q_recv.at[src],
            device_id=(dest, t), device_id_type=MESH,
        )

    def y_copy(way, hop, k, dest):
        rows = pl.ds(pl.multiple_of(k * share, 16), share)
        return pltpu.make_async_remote_copy(
            src_ref=blocks.at[pl.ds(far * 2, 2), rows], dst_ref=blocks.at[pl.ds(far * 2, 2), rows],
            send_sem=y_send.at[way, hop], recv_sem=y_recv.at[way, hop],
            device_id=(s, dest), device_id_type=MESH,
        )

    def w_copy(weight, buf, which, k):
        return pltpu.make_async_copy(
            weight.at[pl.ds(pl.multiple_of(k * fs, fs), fs)], buf, w_sem.at[which]
        )

    def line(way, hop):
        k = t - hop if way == 0 else t + hop
        here = k >= 0 if way == 0 else k < tensors
        onward = up_ok if way == 0 else dn_ok
        dest = t + 1 if way == 0 else t - 1
        return k, here, onward, dest

    def arrive(hop):
        for c in range(chunks):
            for way in range(2):
                k, here, onward, dest = line(way, hop)

                @pl.when(jnp.logical_and(hop > 0, here))
                def _():
                    z_copy(way, hop, c, k, t).wait_recv()

                @pl.when(jnp.logical_and(here, onward))
                def _():
                    z_copy(way, hop + 1, c, k, dest).start()

    def slab_step(hop):
        @pl.when(hop == 0)
        def _():
            for j in range(2):
                m_copy(t, s, far * 2 + j).wait_recv()

        for way in range(2):
            k, here, onward, dest = line(way, hop)

            @pl.when(jnp.logical_and(jnp.logical_and(hop > 0, hop <= reach), here))
            def _():
                l_copy(way, hop, k, t).wait_recv()

            @pl.when(jnp.logical_and(jnp.logical_and(here, onward), hop < reach))
            def _():
                l_copy(way, hop + 1, k, dest).start()

    def y_step(hop):
        for way in range(2):
            k, here, onward, dest = line(way, hop)

            @pl.when(jnp.logical_and(hop > 0, here))
            def _():
                y_copy(way, hop, k, t).wait_recv()

            @pl.when(jnp.logical_and(here, onward))
            def _():
                y_copy(way, hop + 1, k, dest).start()

    def both(hop, what):
        def inner(way, c):
            k = jnp.where(way == 0, t - hop, t + hop)
            fine = jnp.logical_and(jnp.logical_and(k >= 0, k < tensors), jnp.logical_or(hop > 0, way == 0))

            @pl.when(fine)
            def _():
                what(k)
            return c

        lax.fori_loop(0, 2, inner, 0)

    def scale_rows(read, sq, first, gain, rows):
        def step(i, c):
            rr = pl.ds(pl.multiple_of(i * rb, rb), rb)
            x = read(pl.ds(pl.multiple_of(first + i * rb, rb), rb)).astype(jnp.float32)
            square = x * x
            total = square[:, 0:128]
            for j in range(1, fs // 128):
                total = total + square[:, j * 128:(j + 1) * 128]
            sq[pl.ds(pl.multiple_of(first + i * rb, rb), rb), :] += total
            work[rr, :] = (x * gain).astype(jnp.bfloat16)
            return c
        lax.fori_loop(0, rows // rb, step, 0)

    def accumulate(acc, first, rows, buf):
        def step(n, c):
            cols = pl.ds(pl.multiple_of(n * nt, nt), nt)
            acc[first:first + rows, cols] += jnp.dot(
                work[0:rows, :], buf[:, cols], preferred_element_type=jnp.float32
            )
            return c
        lax.fori_loop(0, hid // nt, step, 0)

    def pack(k):
        w_copy(weight_a, wbuf_a, 0, k).start()
        pt = min(fs, 256)

        def column(n, c):
            cols = pl.ds(pl.multiple_of(n * pt, pt), pt)
            outbox[k, :, cols] = jnp.dot(
                dispatch[...], feats[k, :, cols], preferred_element_type=jnp.float32
            ).astype(jnp.bfloat16)
            return c

        lax.fori_loop(0, fs // pt, column, 0)
        own_copy(k).start()

    def far_here(hop):
        return jnp.logical_or(hop == 0, hop > reach)

    def send(k, hop):
        @pl.when(far_here(hop))
        def _():
            for j in range(2):
                m_copy(k, far * 2 + j, s).start()

        def one(r, c):
            dest = lax.rem(s + r, sections)

            @pl.when(dest // 2 != far)
            def _():
                m_copy(k, dest, s).start()
            return c

        lax.fori_loop(1, sections, one, 0)

    def send_blocks(k):
        def one(j, c):
            dest = k * bps + j

            @pl.when(jnp.logical_and(dest != s, dest // 2 != far))
            def _():
                b_copy(dest, s).start()

            @pl.when(dest == s)
            def _():
                own_block().start()
            return c

        lax.fori_loop(0, bps, one, 0)

    def actor(k):
        scale_rows(lambda rr: feats[k, rr, :], sq_a, 0, gain_a[k], tok)
        w_copy(weight_a, wbuf_a, 0, k).wait()
        accumulate(acc_a, 0, tok, wbuf_a)

    def member_near(k):
        w_copy(weight_m, wbuf_m, 1, k).start()
        own_copy(k).wait()

        def take(r, c):
            src = lax.rem(s + r, sections)

            @pl.when(src // 2 != far)
            def _():
                m_copy(k, s, src).wait_recv()
            return c

        lax.fori_loop(1, sections, take, 0)
        scale_rows(lambda rr: inbox[k, rr, :], sq_m, 0, gain_m[k], near)
        w_copy(weight_m, wbuf_m, 1, k).wait()
        accumulate(acc_m, 0, near, wbuf_m)

    def member_far(k, hop):
        w_copy(weight_m, wbuf_m, 1, k).start()

        @pl.when(hop > reach)
        def _():
            for j in range(2):
                m_copy(k, s, far * 2 + j).wait_recv()

        scale_rows(lambda rr: inbox[k, rr, :], sq_m, near, gain_m[k], slots - near)
        w_copy(weight_m, wbuf_m, 1, k).wait()
        accumulate(acc_m, near, slots - near, wbuf_m)

    def g_copy(dest, src):
        return pltpu.make_async_remote_copy(
            src_ref=early, dst_ref=hidden.at[src],
            send_sem=g_send.at[dest], recv_sem=g_recv.at[src],
            device_id=(dest, t), device_id_type=MESH,
        )

    def g_relay(src):
        return pltpu.make_async_remote_copy(
            src_ref=hidden.at[src], dst_ref=hidden.at[src],
            send_sem=g_pass.at[src], recv_sem=g_recv.at[src],
            device_id=(partner, t), device_id_type=MESH,
        )

    beside = (chip + 1 - 2 * lax.rem(chip, 2), chip + 2 - 4 * lax.rem(chip // 2, 2))

    def h_copy(i, src, dest):
        rows = pl.ds(i * half, half)
        return pltpu.make_async_remote_copy(
            src_ref=hidden.at[src, rows], dst_ref=hidden.at[src, rows],
            send_sem=h_send.at[i], recv_sem=h_recv.at[i],
            device_id=(dest, t), device_id_type=MESH,
        )

    def own_hidden():
        return pltpu.make_async_copy(early, hidden.at[s], g_recv.at[s])

    def t_copy(dest, src):
        return pltpu.make_async_remote_copy(
            src_ref=part.at[src], dst_ref=part.at[src],
            send_sem=t_send.at[dest], recv_sem=t_recv.at[src],
            device_id=(s, dest), device_id_type=MESH,
        )

    def u_copy(dest, src):
        return pltpu.make_async_remote_copy(
            src_ref=part_a.at[src], dst_ref=part_a.at[src],
            send_sem=u_send.at[dest], recv_sem=u_recv.at[src],
            device_id=(s, dest), device_id_type=MESH,
        )

    def r_copy(dest, src):
        return pltpu.make_async_remote_copy(
            src_ref=scores.at[dest], dst_ref=back.at[src],
            send_sem=r_send.at[dest], recv_sem=r_recv.at[src],
            device_id=(dest, t), device_id_type=MESH,
        )

    def p_copy(dest, src):
        return pltpu.make_async_remote_copy(
            src_ref=pairs.at[src], dst_ref=pairs.at[src],
            send_sem=p_send.at[dest], recv_sem=p_recv.at[src],
            device_id=(dest, t), device_id_type=MESH,
        )

    def across(x):
        return lax.dot_general(
            jnp.ones((8, 128), jnp.float32), x, (((1,), (1,)), ((), ())),
            precision=lax.Precision.HIGHEST, preferred_element_type=jnp.float32,
        )

    def fold(x):
        total = x[:, 0:128]
        for j in range(1, hid // 128):
            total = total + x[:, j * 128:(j + 1) * 128]
        return total

    def prepare():
        target = jnp.broadcast_to(routes[...], (sections, tok))
        hit = target == lax.broadcasted_iota(jnp.int32, (sections, tok), 0)
        earlier = lax.broadcasted_iota(jnp.int32, (tok, tok), 0) < lax.broadcasted_iota(jnp.int32, (tok, tok), 1)
        placed = jnp.dot(
            hit.astype(jnp.float32).astype(jnp.bfloat16), earlier.astype(jnp.float32).astype(jnp.bfloat16),
            preferred_element_type=jnp.float32,
        )
        code = jnp.where(hit, placed, -1.0)
        slot = lax.broadcasted_iota(jnp.int32, (cap, tok), 0).astype(jnp.float32)
        for m in range(sections):
            here = slot == jnp.broadcast_to(code[m:m + 1, :], (cap, tok))
            dispatch[m * cap:(m + 1) * cap, :] = here.astype(jnp.float32).astype(jnp.bfloat16)

    def mark_ends():
        spot = lax.broadcasted_iota(jnp.int32, (8, tok), 1)
        end = lengths[0, 0]
        marks = (spot == end - 1).astype(jnp.float32)
        for i in range(1, lengths.shape[1]):
            end = end + lengths[0, i]
            marks = jnp.maximum(marks, (spot == end - 1).astype(jnp.float32))
        ended[...] = marks

    def hidden_step():
        def step(i, c):
            rr = pl.ds(pl.multiple_of(i * rb, rb), rb)
            scale = lax.rsqrt(jnp.sum(sq_a[rr, :], axis=1, keepdims=True) / width + epsilon)
            pre = acc_a[rr, :] * scale
            sig = 1.0 / (1.0 + jnp.exp(-pre))
            row = heads_a[...]
            early[rr, :] = (scale * row * (sig * (1.0 + pre * (1.0 - sig)))).astype(jnp.bfloat16)
            lanes[0, rr, :] = fold(pre * sig * row)
            return c

        lax.fori_loop(0, tok // rb, step, 0)
        own_hidden().start()
        g_copy(partner, s).start()

        def send_g(r, c):
            oc = lax.rem(chip + r, chips)

            @pl.when(oc != far)
            def _():
                g_copy(oc * 2 + core, s).start()
            return c

        lax.fori_loop(1, chips, send_g, 0)
        part_a[t] = across(lanes[0, 0:tok, :])

        def send_u(r, c):
            u_copy(lax.rem(t + r, tensors), t).start()
            return c

        lax.fori_loop(1, tensors, send_u, 0)

    def hand_on():
        def relay(r, c):
            oc = lax.rem(chip + r, chips)

            @pl.when(oc != far)
            def _():
                g_copy(s, oc * 2 + core).wait_recv()
                for i in range(2):
                    @pl.when(oc == chips - 1 - beside[i])
                    def _():
                        h_copy(i, oc * 2 + core, beside[i] * 2 + core).start()
                g_relay(oc * 2 + core).start()
            return c

        lax.fori_loop(1, chips, relay, 0)
        own_hidden().wait()

    def hand_far():
        for i in range(2):
            h_copy(i, far * 2 + core, s).wait_recv()
        g_relay(far * 2 + core).start()

    def score_rows(first, rows):
        def step(i, c):
            rr = pl.ds(pl.multiple_of(first + i * rb, rb), rb)
            scale = lax.rsqrt(jnp.sum(sq_m[rr, :], axis=1, keepdims=True) / width + epsilon)
            pre = acc_m[rr, :] * scale
            act = pre * (1.0 / (1.0 + jnp.exp(-pre)))
            lanes[0, rr, :] = fold(act * heads_m[0:1, :])
            lanes[1, rr, :] = fold(act * heads_m[1:2, :])
            return c

        lax.fori_loop(0, rows // rb, step, 0)

    def score_step():
        top = lax.broadcasted_iota(jnp.int32, (8, cap), 0) == 0

        def gather(d, c):
            rr = pl.ds(pl.multiple_of(place(d, s) * cap, cap), cap)
            part[t, d] = jnp.where(top, across(lanes[0, rr, :]), across(lanes[1, rr, :]))
            return c

        lax.fori_loop(0, sections, gather, 0)

        def send_t(r, c):
            t_copy(lax.rem(t + r, tensors), t).start()
            return c

        lax.fori_loop(1, tensors, send_t, 0)
        y_step(tensors - 2)

        def take_t(r, c):
            t_copy(t, lax.rem(t + r, tensors)).wait_recv()
            u_copy(t, lax.rem(t + r, tensors)).wait_recv()
            return c

        lax.fori_loop(1, tensors, take_t, 0)
        scores[...] = lax.fori_loop(1, tensors, lambda k, v: v + part[k], part[0])
        shift = lax.fori_loop(1, tensors, lambda k, v: v + part_a[k], part_a[0])

        def send_r(r, c):
            r_copy(lax.rem(s + r, sections), s).start()
            return c

        lax.fori_loop(1, sections, send_r, 0)
        back[s] = scores[s]

        def take_r(r, c):
            r_copy(s, lax.rem(s + r, sections)).wait_recv()
            return c

        lax.fori_loop(1, sections, take_r, 0)

        def pick(m, v):
            x = back[m]
            hi = x.astype(jnp.bfloat16)
            rest = x - hi.astype(jnp.float32)
            mid = rest.astype(jnp.bfloat16)
            low = (rest - mid.astype(jnp.float32)).astype(jnp.bfloat16)
            rows = dispatch[pl.ds(pl.multiple_of(m * cap, cap), cap), :]
            for piece in (low, mid, hi):
                v = v + jnp.dot(piece, rows, preferred_element_type=jnp.float32)
            return v

        picked = lax.fori_loop(0, sections, pick, jnp.zeros((8, tok), jnp.float32))
        values = jnp.broadcast_to(picked[0:1, :], (8, tok))
        rewards = jnp.broadcast_to(picked[1:2, :], (8, tok))
        stop = ended[...] > 0.5
        total = jnp.where(stop, rewards, pltpu.roll(values, tok - 1, 1)) - values
        carry = jnp.where(stop, 0.0, trace_decay)
        step = 1
        while step < tok:
            total = total + carry * pltpu.roll(total, tok - step, 1)
            carry = carry * pltpu.roll(carry, tok - step, 1)
            step *= 2
        first = lax.broadcasted_iota(jnp.int32, (8, tok), 0) == 0
        pairs[s] = jnp.where(first, total, shift)

        def send_p(r, c):
            p_copy(lax.rem(s + r, sections), s).start()
            return c

        lax.fori_loop(1, sections, send_p, 0)

    arrive(0)
    prepare()
    pack(t)
    send(t, 0)
    acc_m[...] = jnp.zeros_like(acc_m)
    acc_a[...] = jnp.zeros_like(acc_a)
    sq_m[...] = jnp.zeros_like(sq_m)
    sq_a[...] = jnp.zeros_like(sq_a)
    mark_ends()
    actor(t)

    def hop_body(hop, c):
        arrive(hop)

        def ship(k):
            pack(k)
            send(k, hop)
            actor(k)

        @pl.when(hop == 2)
        def _():
            slab_step(0)

        @pl.when(hop == tensors - 1)
        def _():
            for j in range(2):
                q_copy(far * 2 + j, s).start()

        both(hop, ship)
        both(hop - 1, send_blocks)

        @pl.when(hop < tensors - 1)
        def _():
            both(hop - 1, member_near)
        return c

    lax.fori_loop(1, tensors, hop_body, 0)
    hidden_step()
    both(tensors - 1, send_blocks)
    slab_step(1)
    both(tensors - 2, member_near)
    both(tensors - 1, member_near)
    score_rows(0, near)
    member_far(t, 0)
    for j in range(2):
        q_copy(s, far * 2 + j).wait_recv()
    y_step(0)

    def far_body(hop, c):
        @pl.when(hop > 1)
        def _():
            slab_step(hop)
        both(hop, lambda k: member_far(k, hop))

        @pl.when(hop < tensors - 2)
        def _():
            y_step(hop)

        @pl.when(hop == 2)
        def _():
            hand_on()
        return c

    lax.fori_loop(1, tensors, far_body, 0)
    score_rows(near, slots - near)
    score_step()
    hand_far()

    g_copy(s, partner).wait_recv()
    g_copy(partner, s).wait_send()

    def done_g(r, c):
        oc = lax.rem(chip + r, chips)

        @pl.when(oc != far)
        def _():
            g_copy(oc * 2 + core, s).wait_send()

        g_relay(oc * 2 + core).wait_send()
        g_copy(s, oc * 2 + 1 - core).wait_recv()
        return c

    lax.fori_loop(1, chips, done_g, 0)
    for i in range(2):
        h_copy(i, (chips - 1 - beside[i]) * 2 + core, beside[i] * 2 + core).wait_send()

    def done_z(r, c):
        other = lax.rem(t + r, tensors)
        t_copy(other, t).wait_send()
        u_copy(other, t).wait_send()
        return c

    lax.fori_loop(1, tensors, done_z, 0)
    own_block().wait()
    y_step(tensors - 1)
    for j in range(2):
        q_copy(far * 2 + j, s).wait_send()

    def done_s(r, c):
        other = lax.rem(s + r, sections)
        r_copy(other, s).wait_send()
        p_copy(other, s).wait_send()
        p_copy(s, other).wait_recv()

        @pl.when(other // 2 != far)
        def _():
            b_copy(s, other).wait_recv()
            b_copy(other, s).wait_send()

        def sent(k, c):
            gap = jnp.where(k > t, k - t, t - k)

            @pl.when(jnp.logical_or(other // 2 != far, far_here(gap)))
            def _():
                m_copy(k, other, s).wait_send()
            return c

        return lax.fori_loop(0, tensors, sent, c)

    lax.fori_loop(1, sections, done_s, 0)

    def drain(hop, c):
        for way in range(2):
            k, here, onward, dest = line(way, hop)

            @pl.when(jnp.logical_and(here, onward))
            def _():
                y_copy(way, hop + 1, k, dest).wait_send()
                for cc in range(chunks):
                    z_copy(way, hop + 1, cc, k, dest).wait_send()

            @pl.when(jnp.logical_and(jnp.logical_and(here, onward), hop < reach))
            def _():
                l_copy(way, hop + 1, k, dest).wait_send()
        return c

    lax.fori_loop(0, tensors, drain, 0)


def gradient(pairs, gain, blocks, hidden, norm, grad, raw, slope):
    sections, _, tok = pairs.shape
    s = lax.axis_index("section")
    i = pl.program_id(0)

    @pl.when(i == 0)
    def _():
        for j in range(sections):
            raw[0, j:j + 1, :] = pairs[j, 0:1, :]
            raw[1, j:j + 1, :] = pairs[j, 1:2, :]
        total = sections * tok
        value = raw[0]
        center = jnp.sum(jnp.sum(value, axis=1, keepdims=True), axis=0, keepdims=True) / total
        square = jnp.sum(jnp.sum(value * value, axis=1, keepdims=True), axis=0, keepdims=True) / total
        inv = lax.rsqrt(square - center * center + epsilon)
        ratios = jnp.exp(raw[1])
        slope[...] = penalty * (ratios - 1.0) - ratios * ((value - center) * inv)
        norm[...] = (pairs[s][0:1, :] - center) * inv

    wide = hidden.shape[2]
    column = jnp.transpose(jnp.broadcast_to(slope[pl.ds(i, 1), :], (128, tok)))
    right = jnp.concatenate(
        [(hidden[0, :, j * 128:(j + 1) * 128].astype(jnp.float32) * column).astype(jnp.bfloat16) for j in range(wide // 128)],
        axis=1,
    )
    product = lax.dot_general(blocks[0], right, (((0,), (0,)), ((), ())), preferred_element_type=jnp.float32)

    @pl.when(i == 0)
    def _():
        grad[...] = product

    @pl.when(jnp.logical_and(i > 0, i < sections - 1))
    def _():
        grad[...] += product

    @pl.when(i == sections - 1)
    def _():
        rows = product.shape[0]
        own = jnp.transpose(jnp.broadcast_to(gain[s], (128, rows)))
        for j in range(wide // 128):
            cols = slice(j * 128, (j + 1) * 128)
            grad[:, cols] = (grad[:, cols] + product[:, cols]) * own


def body(
    states, lengths, routes, score_gain, score_weight, score_heads,
    actor_gain, actor_weight, actor_heads,
):
    sections = lax.axis_size("section")
    tensors = lax.axis_size("tensor")
    tok, fs = states.shape
    cap = 2 * tok // sections
    slots = sections * cap
    width = score_gain.shape[1]
    hid = actor_weight.shape[1]
    bw = width // sections
    reach = REACH if tensors <= 4 else tensors - 1

    vmem = pl.BlockSpec(memory_space=pltpu.VMEM)
    smem = pl.BlockSpec(memory_space=pltpu.SMEM)
    any_ = pl.BlockSpec(memory_space=pl.ANY)
    f32, bf16 = jnp.float32, jnp.bfloat16
    dma = pltpu.SemaphoreType.DMA
    scores, pairs, blocks, hidden = pl.pallas_call(
        functools.partial(exchange, sections, tensors, cap, reach),
        out_shape=(
            jax.ShapeDtypeStruct((sections, 8, cap), f32),
            jax.ShapeDtypeStruct((sections, 8, tok), f32),
            jax.ShapeDtypeStruct((sections, tok, bw), bf16),
            jax.ShapeDtypeStruct((sections, tok, hid), bf16),
        ),
        in_specs=[any_, vmem, smem, vmem, vmem, any_, any_, vmem, vmem],
        out_specs=(vmem, vmem, any_, any_),
        scratch_shapes=[
            pltpu.VMEM((slots, hid), f32),
            pltpu.VMEM((tok, hid), f32),
            pltpu.VMEM((slots, 128), f32),
            pltpu.VMEM((tok, 128), f32),
            pltpu.VMEM((2, max(slots, tok), 128), f32),
            pltpu.VMEM((tensors, sections, 8, cap), f32),
            pltpu.VMEM((tensors, 8, tok), f32),
            pltpu.VMEM((sections, 8, cap), f32),
            pltpu.VMEM((tok, hid), bf16),
            pltpu.VMEM((tensors, tok, fs), bf16),
            pltpu.VMEM((tensors, slots, fs), bf16),
            pltpu.VMEM((tensors, slots, fs), bf16),
            pltpu.VMEM((max(tok, slots - 2 * cap), fs), bf16),
            pltpu.VMEM((fs, hid), bf16),
            pltpu.VMEM((fs, hid), bf16),
            pltpu.VMEM((slots, tok), bf16),
            pltpu.VMEM((8, tok), f32),
            dma((2, tensors + 1, 2)),
            dma((2, tensors + 1, 2)),
            dma((tensors, sections)),
            dma((tensors, sections)),
            dma((2, tensors + 1)),
            dma((2, tensors + 1)),
            dma((sections,)),
            dma((sections,)),
            dma((1,)),
            dma((2,)),
            dma((tensors,)),
            dma((tensors,)),
            dma((tensors,)),
            dma((tensors,)),
            dma((sections,)),
            dma((sections,)),
            dma((sections,)),
            dma((sections,)),
            dma((sections,)),
            dma((sections,)),
            dma((sections,)),
            dma((2,)),
            dma((2,)),
            dma((sections,)),
            dma((sections,)),
            dma((2, tensors + 1)),
            dma((2, tensors + 1)),
        ],
        compiler_params=pltpu.CompilerParams(
            collective_id=0, has_side_effects=True, vmem_limit_bytes=67043328
        ),
    )(
        states, routes.reshape(1, tok), lengths, score_gain[0].reshape(tensors, 1, fs),
        actor_gain.reshape(tensors, 1, fs), score_weight[0], actor_weight,
        jnp.transpose(score_heads[0]), actor_heads[None, :],
    )

    norm, actor_grad = pl.pallas_call(
        gradient,
        grid=(sections,),
        out_shape=(jax.ShapeDtypeStruct((1, tok), f32), jax.ShapeDtypeStruct((bw, hid), f32)),
        in_specs=[
            vmem, vmem,
            pl.BlockSpec((1, tok, bw), lambda i: (i, 0, 0)),
            pl.BlockSpec((1, tok, hid), lambda i: (i, 0, 0)),
        ],
        out_specs=(
            pl.BlockSpec((1, tok), lambda i: (0, 0)),
            pl.BlockSpec((bw, hid), lambda i: (0, 0)),
        ),
        scratch_shapes=[pltpu.VMEM((2, sections, tok), f32), pltpu.VMEM((sections, tok), f32)],
        compiler_params=pltpu.CompilerParams(vmem_limit_bytes=50 * 1024 * 1024),
    )(pairs, actor_gain.reshape(sections, 1, bw), blocks, hidden)
    packed_scores = jnp.transpose(scores[:, :2], (1, 0, 2)).reshape(2, slots)
    return (packed_scores, norm[0], actor_grad)


REACH = 2


def solution(mesh):
    in_specs = (
        P("section", "tensor"),
        P("section", None),
        P("section", None),
        P("section", None),
        P("section", None, "tensor"),
        P("section", "tensor", None),
        P(),
        P(None, "tensor"),
        P("tensor"),
    )
    out_specs = (P(None, "section"), P("section"), P("section", "tensor"))
    return jax.shard_map(body, mesh=mesh, in_specs=in_specs, out_specs=out_specs, check_vma=False)
```

```python
import functools
import jax
import jax.numpy as jnp
from jax import lax
from jax.experimental import pallas as pl
from jax.experimental.pallas import tpu as pltpu
from jax.sharding import PartitionSpec as P

epsilon = 1e-05
trace_decay = 0.95
penalty = 0.1
MESH = pl.DeviceIdType.MESH


def exchange(
    sections, tensors, cap,
    states, routes, lengths, gain_m, gain_a, weight_m, weight_a, heads_m, heads_a,
    scores, pairs, blocks, hidden,
    acc_m, acc_a, sq_m, sq_a, lanes, part, part_a, back, early, feats, outbox, inbox, work, wbuf_m, wbuf_a,
    dispatch, ended,
    z_send, z_recv, m_send, m_recv, l_send, l_recv, b_send, b_recv, loc_sem, w_sem,
    t_send, t_recv, u_send, u_recv, r_send, r_recv, p_send, p_recv, g_send, g_recv, g_pass,
    h_send, h_recv, q_send, q_recv, y_send, y_recv,
):
    s = lax.axis_index("section")
    t = lax.axis_index("tensor")
    tok, fs = states.shape
    slots = sections * cap
    bw = blocks.shape[2]
    hid = acc_m.shape[1]
    nt = min(hid, 256)
    uw = fs // 2
    pieces = bw // uw
    half = tok // 2
    up_ok = t + 1 < tensors
    dn_ok = t > 0
    chips = sections // 2
    chip = s // 2
    core = lax.rem(s, 2)
    partner = s + 1 - 2 * core
    far = chips - 1 - chip
    near = slots - 2 * cap
    share = max(16, 5 * tok // 8 // tensors // 16 * 16)
    shared = share * tensors
    width = fs * tensors
    rb = 64

    def place(src, dest):
        return lax.rem(src // 2 + dest // 2, chips) * 2 + lax.rem(src, 2)

    def load(c):
        return pltpu.make_async_copy(states.at[:, pl.ds(c * uw, uw)], feats.at[2 * t + c], loc_sem.at[c])

    for c in range(2):
        load(c).start()

    barrier = pltpu.get_barrier_semaphore()

    def greet(r, c):
        pl.semaphore_signal(barrier, inc=1, device_id=(lax.rem(s + r, sections), t), device_id_type=MESH)
        return c

    lax.fori_loop(1, sections, greet, 0)

    def greet_z(r, c):
        pl.semaphore_signal(barrier, inc=1, device_id=(s, lax.rem(t + r, tensors)), device_id_type=MESH)
        return c

    lax.fori_loop(1, tensors, greet_z, 0)
    pl.semaphore_wait(barrier, sections - 1 + tensors - 1)
    for c in range(2):
        load(c).wait()

    parts = 2
    rows_z = tok // parts

    def z_copy(way, hop, c, h, shard, dest):
        rows = pl.ds(h * rows_z, rows_z)
        return pltpu.make_async_remote_copy(
            src_ref=feats.at[2 * shard + c, rows], dst_ref=feats.at[2 * shard + c, rows],
            send_sem=z_send.at[way, hop, c, h], recv_sem=z_recv.at[way, hop, c, h],
            device_id=(s, dest), device_id_type=MESH,
        )

    def m_copy(k, dest, src):
        return pltpu.make_async_remote_copy(
            src_ref=outbox.at[k, pl.ds(pl.multiple_of(dest * cap, cap), cap)],
            dst_ref=inbox.at[k, pl.ds(pl.multiple_of(place(src, dest) * cap, cap), cap)],
            send_sem=m_send.at[k, dest], recv_sem=m_recv.at[k, src],
            device_id=(dest, t), device_id_type=MESH,
        )

    def own_copy(k):
        return pltpu.make_async_copy(
            outbox.at[k, pl.ds(pl.multiple_of(s * cap, cap), cap)],
            inbox.at[k, pl.ds(pl.multiple_of(place(s, s) * cap, cap), cap)],
            m_recv.at[k, s],
        )

    def l_copy(way, hop, c, shard, dest):
        rows = pl.ds(near, 2 * cap)
        return pltpu.make_async_remote_copy(
            src_ref=inbox.at[2 * shard + c, rows], dst_ref=inbox.at[2 * shard + c, rows],
            send_sem=l_send.at[way, hop, c], recv_sem=l_recv.at[way, hop, c],
            device_id=(s, dest), device_id_type=MESH,
        )

    def b_dst(src, u, row, count):
        return blocks.at[src, pl.ds(row, count), pl.ds(pl.multiple_of(lax.rem(u, pieces) * uw, uw), uw)]

    def b_copy(u, src, first):
        dest = u // pieces
        piece = lax.rem(u, pieces)
        return pltpu.make_async_remote_copy(
            src_ref=feats.at[u, pl.ds(first, tok - first)], dst_ref=b_dst(src, u, first, tok - first),
            send_sem=b_send.at[dest, piece], recv_sem=b_recv.at[src, piece],
            device_id=(dest, t), device_id_type=MESH,
        )

    def own_block(u):
        return pltpu.make_async_copy(feats.at[u], b_dst(s, u, 0, tok), b_recv.at[s, lax.rem(u, pieces)])

    def q_copy(u, src):
        dest = u // pieces
        piece = lax.rem(u, pieces)
        row = pl.multiple_of(t * share, 16)
        return pltpu.make_async_remote_copy(
            src_ref=feats.at[u, pl.ds(row, share)], dst_ref=b_dst(src, u, row, share),
            send_sem=q_send.at[dest, piece], recv_sem=q_recv.at[src, piece],
            device_id=(dest, t), device_id_type=MESH,
        )

    def y_copy(way, hop, k, dest):
        rows = pl.ds(pl.multiple_of(k * share, 16), share)
        return pltpu.make_async_remote_copy(
            src_ref=blocks.at[pl.ds(far * 2, 2), rows], dst_ref=blocks.at[pl.ds(far * 2, 2), rows],
            send_sem=y_send.at[way, hop], recv_sem=y_recv.at[way, hop],
            device_id=(s, dest), device_id_type=MESH,
        )

    def w_copy(weight, buf, which, k):
        return pltpu.make_async_copy(
            weight.at[pl.ds(pl.multiple_of(k * uw, uw), uw)], buf, w_sem.at[which]
        )

    def line(way, hop):
        k = t - hop if way == 0 else t + hop
        here = k >= 0 if way == 0 else k < tensors
        onward = up_ok if way == 0 else dn_ok
        dest = t + 1 if way == 0 else t - 1
        return k, here, onward, dest

    def arrive(hop, c):
        for h in range(parts):
            for way in range(2):
                k, here, onward, dest = line(way, hop)

                @pl.when(jnp.logical_and(hop > 0, here))
                def _():
                    z_copy(way, hop, c, h, k, t).wait_recv()

                @pl.when(jnp.logical_and(here, onward))
                def _():
                    z_copy(way, hop + 1, c, h, k, dest).start()

    def slab_first(c):
        for j in range(2):
            m_copy(2 * t + c, s, far * 2 + j).wait_recv()
        for way in range(2):
            k, here, onward, dest = line(way, 0)

            @pl.when(onward)
            def _():
                l_copy(way, 1, c, t, dest).start()

    def slab_pass(hop, c):
        for way in range(2):
            k, here, onward, dest = line(way, hop)

            @pl.when(jnp.logical_and(here, onward))
            def _():
                l_copy(way, hop, c, k, t).wait_recv()
                l_copy(way, hop + 1, c, k, dest).start()

    def slab_end(hop, c):
        for way in range(2):
            k, here, onward, dest = line(way, hop)

            @pl.when(jnp.logical_and(here, jnp.logical_not(onward)))
            def _():
                l_copy(way, hop, c, k, t).wait_recv()

    def y_step(hop):
        for way in range(2):
            k, here, onward, dest = line(way, hop)

            @pl.when(jnp.logical_and(hop > 0, here))
            def _():
                y_copy(way, hop, k, t).wait_recv()

            @pl.when(jnp.logical_and(here, onward))
            def _():
                y_copy(way, hop + 1, k, dest).start()

    def both(hop, c, what):
        def inner(way, carry):
            k = jnp.where(way == 0, t - hop, t + hop)
            fine = jnp.logical_and(jnp.logical_and(k >= 0, k < tensors), jnp.logical_or(hop > 0, way == 0))

            @pl.when(fine)
            def _():
                what(2 * k + c)
            return carry

        lax.fori_loop(0, 2, inner, 0)

    def scale_rows(read, sq, first, gain, rows):
        def step(i, c):
            rr = pl.ds(pl.multiple_of(i * rb, rb), rb)
            x = read(pl.ds(pl.multiple_of(first + i * rb, rb), rb)).astype(jnp.float32)
            square = x * x
            total = square[:, 0:128]
            for j in range(1, uw // 128):
                total = total + square[:, j * 128:(j + 1) * 128]
            sq[pl.ds(pl.multiple_of(first + i * rb, rb), rb), :] += total
            work[rr, :] = (x * gain).astype(jnp.bfloat16)
            return c
        lax.fori_loop(0, rows // rb, step, 0)

    def accumulate(acc, first, rows, buf):
        def step(n, c):
            cols = pl.ds(pl.multiple_of(n * nt, nt), nt)
            acc[first:first + rows, cols] += jnp.dot(
                work[0:rows, :], buf[:, cols], preferred_element_type=jnp.float32
            )
            return c
        lax.fori_loop(0, hid // nt, step, 0)

    def pack(k):
        pt = min(uw, 256)

        def column(n, c):
            cols = pl.ds(pl.multiple_of(n * pt, pt), pt)
            outbox[k, :, cols] = jnp.dot(
                dispatch[...], feats[k, :, cols], preferred_element_type=jnp.float32
            ).astype(jnp.bfloat16)
            return c

        lax.fori_loop(0, uw // pt, column, 0)
        own_copy(k).start()

    def send(u, hop):
        @pl.when(hop == 0)
        def _():
            for j in range(2):
                m_copy(u, far * 2 + j, s).start()

        def one(r, c):
            dest = lax.rem(s + r, sections)

            @pl.when(dest // 2 != far)
            def _():
                m_copy(u, dest, s).start()
            return c

        lax.fori_loop(1, sections, one, 0)

    def send_block(u):
        dest = u // pieces

        @pl.when(dest == s)
        def _():
            own_block(u).start()

        @pl.when(jnp.logical_and(dest != s, dest // 2 != far))
        def _():
            b_copy(u, s, 0).start()

        @pl.when(dest // 2 == far)
        def _():
            q_copy(u, s).start()
            if shared < tok:
                b_copy(u, s, shared).start()

    def fetch(k):
        w_copy(weight_a, wbuf_a, 0, k).start()

    def actor(k):
        scale_rows(lambda rr: feats[k, rr, :], sq_a, 0, gain_a[k], tok)
        w_copy(weight_a, wbuf_a, 0, k).wait()
        accumulate(acc_a, 0, tok, wbuf_a)

    def member_near(k):
        w_copy(weight_m, wbuf_m, 1, k).start()
        own_copy(k).wait()

        def take(r, c):
            src = lax.rem(s + r, sections)

            @pl.when(src // 2 != far)
            def _():
                m_copy(k, s, src).wait_recv()
            return c

        lax.fori_loop(1, sections, take, 0)
        scale_rows(lambda rr: inbox[k, rr, :], sq_m, 0, gain_m[k], near)
        w_copy(weight_m, wbuf_m, 1, k).wait()
        accumulate(acc_m, 0, near, wbuf_m)

    def member_far(k):
        w_copy(weight_m, wbuf_m, 1, k).start()
        scale_rows(lambda rr: inbox[k, rr, :], sq_m, near, gain_m[k], slots - near)
        w_copy(weight_m, wbuf_m, 1, k).wait()
        accumulate(acc_m, near, slots - near, wbuf_m)

    def g_copy(dest, src):
        return pltpu.make_async_remote_copy(
            src_ref=early, dst_ref=hidden.at[src],
            send_sem=g_send.at[dest], recv_sem=g_recv.at[src],
            device_id=(dest, t), device_id_type=MESH,
        )

    def g_relay(src):
        return pltpu.make_async_remote_copy(
            src_ref=hidden.at[src], dst_ref=hidden.at[src],
            send_sem=g_pass.at[src], recv_sem=g_recv.at[src],
            device_id=(partner, t), device_id_type=MESH,
        )

    beside = (chip + 1 - 2 * lax.rem(chip, 2), chip + 2 - 4 * lax.rem(chip // 2, 2))

    def h_copy(i, src, dest):
        rows = pl.ds(i * half, half)
        return pltpu.make_async_remote_copy(
            src_ref=hidden.at[src, rows], dst_ref=hidden.at[src, rows],
            send_sem=h_send.at[i], recv_sem=h_recv.at[i],
            device_id=(dest, t), device_id_type=MESH,
        )

    def own_hidden():
        return pltpu.make_async_copy(early, hidden.at[s], g_recv.at[s])

    def t_copy(dest, src):
        return pltpu.make_async_remote_copy(
            src_ref=part.at[src], dst_ref=part.at[src],
            send_sem=t_send.at[dest], recv_sem=t_recv.at[src],
            device_id=(s, dest), device_id_type=MESH,
        )

    def u_copy(dest, src):
        return pltpu.make_async_remote_copy(
            src_ref=part_a.at[src], dst_ref=part_a.at[src],
            send_sem=u_send.at[dest], recv_sem=u_recv.at[src],
            device_id=(s, dest), device_id_type=MESH,
        )

    def r_copy(dest, src):
        return pltpu.make_async_remote_copy(
            src_ref=scores.at[dest], dst_ref=back.at[src],
            send_sem=r_send.at[dest], recv_sem=r_recv.at[src],
            device_id=(dest, t), device_id_type=MESH,
        )

    def p_copy(dest, src):
        return pltpu.make_async_remote_copy(
            src_ref=pairs.at[src], dst_ref=pairs.at[src],
            send_sem=p_send.at[dest], recv_sem=p_recv.at[src],
            device_id=(dest, t), device_id_type=MESH,
        )

    def across(x):
        return lax.dot_general(
            jnp.ones((8, 128), jnp.float32), x, (((1,), (1,)), ((), ())),
            precision=lax.Precision.HIGHEST, preferred_element_type=jnp.float32,
        )

    def fold(x):
        total = x[:, 0:128]
        for j in range(1, hid // 128):
            total = total + x[:, j * 128:(j + 1) * 128]
        return total

    def prepare():
        target = jnp.broadcast_to(routes[...], (sections, tok))
        hit = target == lax.broadcasted_iota(jnp.int32, (sections, tok), 0)
        earlier = lax.broadcasted_iota(jnp.int32, (tok, tok), 0) < lax.broadcasted_iota(jnp.int32, (tok, tok), 1)
        placed = jnp.dot(
            hit.astype(jnp.float32).astype(jnp.bfloat16), earlier.astype(jnp.float32).astype(jnp.bfloat16),
            preferred_element_type=jnp.float32,
        )
        code = jnp.where(hit, placed, -1.0)
        slot = lax.broadcasted_iota(jnp.int32, (cap, tok), 0).astype(jnp.float32)
        for m in range(sections):
            here = slot == jnp.broadcast_to(code[m:m + 1, :], (cap, tok))
            dispatch[m * cap:(m + 1) * cap, :] = here.astype(jnp.float32).astype(jnp.bfloat16)

    def mark_ends():
        spot = lax.broadcasted_iota(jnp.int32, (8, tok), 1)
        end = lengths[0, 0]
        marks = (spot == end - 1).astype(jnp.float32)
        for i in range(1, lengths.shape[1]):
            end = end + lengths[0, i]
            marks = jnp.maximum(marks, (spot == end - 1).astype(jnp.float32))
        ended[...] = marks

    def hidden_step():
        def step(i, c):
            rr = pl.ds(pl.multiple_of(i * rb, rb), rb)
            scale = lax.rsqrt(jnp.sum(sq_a[rr, :], axis=1, keepdims=True) / width + epsilon)
            pre = acc_a[rr, :] * scale
            sig = 1.0 / (1.0 + jnp.exp(-pre))
            row = heads_a[...]
            early[rr, :] = (scale * row * (sig * (1.0 + pre * (1.0 - sig)))).astype(jnp.bfloat16)
            lanes[0, rr, :] = fold(pre * sig * row)
            return c

        lax.fori_loop(0, tok // rb, step, 0)
        own_hidden().start()
        g_copy(partner, s).start()

        def send_g(r, c):
            oc = lax.rem(chip + r, chips)

            @pl.when(oc != far)
            def _():
                g_copy(oc * 2 + core, s).start()
            return c

        lax.fori_loop(1, chips, send_g, 0)
        part_a[t] = across(lanes[0, 0:tok, :])

        def send_u(r, c):
            u_copy(lax.rem(t + r, tensors), t).start()
            return c

        lax.fori_loop(1, tensors, send_u, 0)

    def hand_on():
        def relay(r, c):
            oc = lax.rem(chip + r, chips)

            @pl.when(oc != far)
            def _():
                g_copy(s, oc * 2 + core).wait_recv()
                for i in range(2):
                    @pl.when(oc == chips - 1 - beside[i])
                    def _():
                        h_copy(i, oc * 2 + core, beside[i] * 2 + core).start()
                g_relay(oc * 2 + core).start()
            return c

        lax.fori_loop(1, chips, relay, 0)
        own_hidden().wait()

    def hand_far():
        for i in range(2):
            h_copy(i, far * 2 + core, s).wait_recv()
        g_relay(far * 2 + core).start()

    def score_rows(first, rows):
        def step(i, c):
            rr = pl.ds(pl.multiple_of(first + i * rb, rb), rb)
            scale = lax.rsqrt(jnp.sum(sq_m[rr, :], axis=1, keepdims=True) / width + epsilon)
            pre = acc_m[rr, :] * scale
            act = pre * (1.0 / (1.0 + jnp.exp(-pre)))
            lanes[0, rr, :] = fold(act * heads_m[0:1, :])
            lanes[1, rr, :] = fold(act * heads_m[1:2, :])
            return c

        lax.fori_loop(0, rows // rb, step, 0)

    def score_step():
        top = lax.broadcasted_iota(jnp.int32, (8, cap), 0) == 0

        def gather(d, c):
            rr = pl.ds(pl.multiple_of(place(d, s) * cap, cap), cap)
            part[t, d] = jnp.where(top, across(lanes[0, rr, :]), across(lanes[1, rr, :]))
            return c

        lax.fori_loop(0, sections, gather, 0)

        def send_t(r, c):
            t_copy(lax.rem(t + r, tensors), t).start()
            return c

        lax.fori_loop(1, tensors, send_t, 0)
        y_step(tensors - 2)

        def take_t(r, c):
            t_copy(t, lax.rem(t + r, tensors)).wait_recv()
            u_copy(t, lax.rem(t + r, tensors)).wait_recv()
            return c

        lax.fori_loop(1, tensors, take_t, 0)
        scores[...] = lax.fori_loop(1, tensors, lambda k, v: v + part[k], part[0])
        shift = lax.fori_loop(1, tensors, lambda k, v: v + part_a[k], part_a[0])

        def send_r(r, c):
            r_copy(lax.rem(s + r, sections), s).start()
            return c

        lax.fori_loop(1, sections, send_r, 0)
        back[s] = scores[s]

        def take_r(r, c):
            r_copy(s, lax.rem(s + r, sections)).wait_recv()
            return c

        lax.fori_loop(1, sections, take_r, 0)

        def pick(m, v):
            x = back[m]
            hi = x.astype(jnp.bfloat16)
            rest = x - hi.astype(jnp.float32)
            mid = rest.astype(jnp.bfloat16)
            low = (rest - mid.astype(jnp.float32)).astype(jnp.bfloat16)
            rows = dispatch[pl.ds(pl.multiple_of(m * cap, cap), cap), :]
            for piece in (low, mid, hi):
                v = v + jnp.dot(piece, rows, preferred_element_type=jnp.float32)
            return v

        picked = lax.fori_loop(0, sections, pick, jnp.zeros((8, tok), jnp.float32))
        values = jnp.broadcast_to(picked[0:1, :], (8, tok))
        rewards = jnp.broadcast_to(picked[1:2, :], (8, tok))
        stop = ended[...] > 0.5
        total = jnp.where(stop, rewards, pltpu.roll(values, tok - 1, 1)) - values
        carry = jnp.where(stop, 0.0, trace_decay)
        step = 1
        while step < tok:
            total = total + carry * pltpu.roll(total, tok - step, 1)
            carry = carry * pltpu.roll(carry, tok - step, 1)
            step *= 2
        first = lax.broadcasted_iota(jnp.int32, (8, tok), 0) == 0
        pairs[s] = jnp.where(first, total, shift)

        def send_p(r, c):
            p_copy(lax.rem(s + r, sections), s).start()
            return c

        lax.fori_loop(1, sections, send_p, 0)

    arrive(0, 0)
    prepare()

    def ship(u, hop):
        pack(u)
        send(u, hop)
        send_block(u)

    def turn_of(j):
        return lax.rem(j, tensors), j // tensors

    fetch(2 * t)
    ship(2 * t, 0)
    ship(2 * t + 1, 0)
    acc_m[...] = jnp.zeros_like(acc_m)
    acc_a[...] = jnp.zeros_like(acc_a)
    sq_m[...] = jnp.zeros_like(sq_m)
    sq_a[...] = jnp.zeros_like(sq_a)
    mark_ends()
    actor(2 * t)
    lag = 6

    def turn(j, carry):
        hop, c = turn_of(j)
        arrive(hop, c)

        @pl.when(j >= 2 * tensors - 2)
        def _():
            slab_first(j - (2 * tensors - 2))

        def take(u):
            fetch(u)

            @pl.when(hop > 0)
            def _():
                ship(u, hop)

            actor(u)

        both(hop, c, take)

        @pl.when(j >= lag)
        def _():
            both(*turn_of(j - lag), member_near)
        return carry

    lax.fori_loop(1, 2 * tensors, turn, 0)
    hidden_step()

    def passes(j, carry):
        slab_pass(j // 2, lax.rem(j, 2))
        return carry

    lax.fori_loop(2, 4, passes, 0)

    def rest(j, carry):
        both(*turn_of(j), member_near)
        return carry

    cut = 2 * tensors - 3
    lax.fori_loop(2 * tensors - lag, cut, rest, 0)
    lax.fori_loop(4, 2 * tensors - 2, passes, 0)
    lax.fori_loop(cut, 2 * tensors, rest, 0)
    score_rows(0, near)

    def far_rows(j, carry):
        hop, c = j // 2, lax.rem(j, 2)

        @pl.when(hop > 0)
        def _():
            slab_end(hop, c)

        both(hop, c, member_far)

        @pl.when(j == 3)
        def _():
            def shares(p, carry):
                for i in range(2):
                    q_copy(s * pieces + p, far * 2 + i).wait_recv()
                return carry

            lax.fori_loop(0, pieces, shares, 0)
            y_step(0)
            hand_on()

        @pl.when(jnp.logical_and(jnp.logical_and(hop > 1, c == 1), hop < tensors - 1))
        def _():
            y_step(hop - 1)
        return carry

    lax.fori_loop(0, 2 * tensors, far_rows, 0)
    score_rows(near, slots - near)
    score_step()
    hand_far()

    g_copy(s, partner).wait_recv()
    g_copy(partner, s).wait_send()

    def done_g(r, c):
        oc = lax.rem(chip + r, chips)

        @pl.when(oc != far)
        def _():
            g_copy(oc * 2 + core, s).wait_send()

        g_relay(oc * 2 + core).wait_send()
        g_copy(s, oc * 2 + 1 - core).wait_recv()
        return c

    lax.fori_loop(1, chips, done_g, 0)
    for i in range(2):
        h_copy(i, (chips - 1 - beside[i]) * 2 + core, beside[i] * 2 + core).wait_send()

    def done_z(r, c):
        other = lax.rem(t + r, tensors)
        t_copy(other, t).wait_send()
        u_copy(other, t).wait_send()
        return c

    lax.fori_loop(1, tensors, done_z, 0)
    y_step(tensors - 1)

    def done_b(p, carry):
        own_block(s * pieces + p).wait()
        for i in range(2):
            q_copy((far * 2 + i) * pieces + p, s).wait_send()

        def one(r, carry):
            other = lax.rem(s + r, sections)

            @pl.when(other // 2 != far)
            def _():
                b_copy(s * pieces + p, other, 0).wait_recv()
                b_copy(other * pieces + p, s, 0).wait_send()

            if shared < tok:
                @pl.when(other // 2 == far)
                def _():
                    b_copy(s * pieces + p, other, shared).wait_recv()
                    b_copy(other * pieces + p, s, shared).wait_send()
            return carry

        return lax.fori_loop(1, sections, one, carry)

    lax.fori_loop(0, pieces, done_b, 0)

    def done_s(r, c):
        other = lax.rem(s + r, sections)
        r_copy(other, s).wait_send()
        p_copy(other, s).wait_send()
        p_copy(s, other).wait_recv()

        def sent(u, c):
            @pl.when(jnp.logical_or(other // 2 != far, u // 2 == t))
            def _():
                m_copy(u, other, s).wait_send()
            return c

        return lax.fori_loop(0, 2 * tensors, sent, c)

    lax.fori_loop(1, sections, done_s, 0)

    def drain(hop, carry):
        for way in range(2):
            k, here, onward, dest = line(way, hop)

            @pl.when(jnp.logical_and(here, onward))
            def _():
                y_copy(way, hop + 1, k, dest).wait_send()
                for c in range(2):
                    for h in range(parts):
                        z_copy(way, hop + 1, c, h, k, dest).wait_send()
                    l_copy(way, hop + 1, c, k, dest).wait_send()
        return carry

    lax.fori_loop(0, tensors, drain, 0)


def gradient(pairs, gain, blocks, hidden, norm, grad, raw, slope):
    sections, _, tok = pairs.shape
    s = lax.axis_index("section")
    i = pl.program_id(0)

    @pl.when(i == 0)
    def _():
        for j in range(sections):
            raw[0, j:j + 1, :] = pairs[j, 0:1, :]
            raw[1, j:j + 1, :] = pairs[j, 1:2, :]
        total = sections * tok
        value = raw[0]
        center = jnp.sum(jnp.sum(value, axis=1, keepdims=True), axis=0, keepdims=True) / total
        square = jnp.sum(jnp.sum(value * value, axis=1, keepdims=True), axis=0, keepdims=True) / total
        inv = lax.rsqrt(square - center * center + epsilon)
        ratios = jnp.exp(raw[1])
        slope[...] = penalty * (ratios - 1.0) - ratios * ((value - center) * inv)
        norm[...] = (pairs[s][0:1, :] - center) * inv

    per, _, wide = hidden.shape
    last = sections // per - 1
    def scaled(p):
        column = jnp.transpose(jnp.broadcast_to(slope[pl.ds(i * per + p, 1), :], (128, tok)))
        return jnp.concatenate(
            [
                (hidden[p, :, j * 128:(j + 1) * 128].astype(jnp.float32) * column).astype(jnp.bfloat16)
                for j in range(wide // 128)
            ],
            axis=1,
        )

    right = jnp.concatenate([scaled(p) for p in range(per)], axis=0)
    left = blocks[...].reshape(per * tok, blocks.shape[2])
    product = lax.dot_general(left, right, (((0,), (0,)), ((), ())), preferred_element_type=jnp.float32)

    @pl.when(i == 0)
    def _():
        grad[...] = product

    @pl.when(jnp.logical_and(i > 0, i < last))
    def _():
        grad[...] += product

    @pl.when(i == last)
    def _():
        rows = product.shape[0]
        own = jnp.transpose(jnp.broadcast_to(gain[s], (128, rows)))
        for j in range(wide // 128):
            cols = slice(j * 128, (j + 1) * 128)
            grad[:, cols] = (grad[:, cols] + product[:, cols]) * own


def body(
    states, lengths, routes, score_gain, score_weight, score_heads,
    actor_gain, actor_weight, actor_heads,
):
    sections = lax.axis_size("section")
    tensors = lax.axis_size("tensor")
    tok, fs = states.shape
    cap = 2 * tok // sections
    slots = sections * cap
    width = score_gain.shape[1]
    hid = actor_weight.shape[1]
    bw = width // sections
    uw = fs // 2
    pieces = bw // uw

    vmem = pl.BlockSpec(memory_space=pltpu.VMEM)
    smem = pl.BlockSpec(memory_space=pltpu.SMEM)
    any_ = pl.BlockSpec(memory_space=pl.ANY)
    f32, bf16 = jnp.float32, jnp.bfloat16
    dma = pltpu.SemaphoreType.DMA
    scores, pairs, blocks, hidden = pl.pallas_call(
        functools.partial(exchange, sections, tensors, cap),
        out_shape=(
            jax.ShapeDtypeStruct((sections, 8, cap), f32),
            jax.ShapeDtypeStruct((sections, 8, tok), f32),
            jax.ShapeDtypeStruct((sections, tok, bw), bf16),
            jax.ShapeDtypeStruct((sections, tok, hid), bf16),
        ),
        in_specs=[any_, vmem, smem, vmem, vmem, any_, any_, vmem, vmem],
        out_specs=(vmem, vmem, any_, any_),
        scratch_shapes=[
            pltpu.VMEM((slots, hid), f32),
            pltpu.VMEM((tok, hid), f32),
            pltpu.VMEM((slots, 128), f32),
            pltpu.VMEM((tok, 128), f32),
            pltpu.VMEM((2, max(slots, tok), 128), f32),
            pltpu.VMEM((tensors, sections, 8, cap), f32),
            pltpu.VMEM((tensors, 8, tok), f32),
            pltpu.VMEM((sections, 8, cap), f32),
            pltpu.VMEM((tok, hid), bf16),
            pltpu.VMEM((2 * tensors, tok, uw), bf16),
            pltpu.VMEM((2 * tensors, slots, uw), bf16),
            pltpu.VMEM((2 * tensors, slots, uw), bf16),
            pltpu.VMEM((max(tok, slots - 2 * cap), uw), bf16),
            pltpu.VMEM((uw, hid), bf16),
            pltpu.VMEM((uw, hid), bf16),
            pltpu.VMEM((slots, tok), bf16),
            pltpu.VMEM((8, tok), f32),
            dma((2, tensors + 1, 2, 2)),
            dma((2, tensors + 1, 2, 2)),
            dma((2 * tensors, sections)),
            dma((2 * tensors, sections)),
            dma((2, tensors + 1, 2)),
            dma((2, tensors + 1, 2)),
            dma((sections, pieces)),
            dma((sections, pieces)),
            dma((2,)),
            dma((2,)),
            dma((tensors,)),
            dma((tensors,)),
            dma((tensors,)),
            dma((tensors,)),
            dma((sections,)),
            dma((sections,)),
            dma((sections,)),
            dma((sections,)),
            dma((sections,)),
            dma((sections,)),
            dma((sections,)),
            dma((2,)),
            dma((2,)),
            dma((sections, pieces)),
            dma((sections, pieces)),
            dma((2, tensors + 1)),
            dma((2, tensors + 1)),
        ],
        compiler_params=pltpu.CompilerParams(
            collective_id=0, has_side_effects=True, vmem_limit_bytes=67043328
        ),
    )(
        states, routes.reshape(1, tok), lengths, score_gain[0].reshape(2 * tensors, 1, uw),
        actor_gain.reshape(2 * tensors, 1, uw), score_weight[0], actor_weight,
        jnp.transpose(score_heads[0]), actor_heads[None, :],
    )

    norm, actor_grad = pl.pallas_call(
        gradient,
        grid=(sections // 2,),
        out_shape=(jax.ShapeDtypeStruct((1, tok), f32), jax.ShapeDtypeStruct((bw, hid), f32)),
        in_specs=[
            vmem, vmem,
            pl.BlockSpec((2, tok, bw), lambda i: (i, 0, 0)),
            pl.BlockSpec((2, tok, hid), lambda i: (i, 0, 0)),
        ],
        out_specs=(
            pl.BlockSpec((1, tok), lambda i: (0, 0)),
            pl.BlockSpec((bw, hid), lambda i: (0, 0)),
        ),
        scratch_shapes=[pltpu.VMEM((2, sections, tok), f32), pltpu.VMEM((sections, tok), f32)],
        compiler_params=pltpu.CompilerParams(vmem_limit_bytes=50 * 1024 * 1024),
    )(pairs, actor_gain.reshape(sections, 1, bw), blocks, hidden)
    packed_scores = jnp.transpose(scores[:, :2], (1, 0, 2)).reshape(2, slots)
    return (packed_scores, norm[0], actor_grad)


def solution(mesh):
    in_specs = (
        P("section", "tensor"),
        P("section", None),
        P("section", None),
        P("section", None),
        P("section", None, "tensor"),
        P("section", "tensor", None),
        P(),
        P(None, "tensor"),
        P("tensor"),
    )
    out_specs = (P(None, "section"), P("section"), P("section", "tensor"))
    return jax.shard_map(body, mesh=mesh, in_specs=in_specs, out_specs=out_specs, check_vma=False)
```

```python
import functools
import jax
import jax.numpy as jnp
from jax import lax
from jax.experimental import pallas as pl
from jax.experimental.pallas import tpu as pltpu
from jax.sharding import PartitionSpec as P

epsilon = 1e-05
trace_decay = 0.95
penalty = 0.1
MESH = pl.DeviceIdType.MESH


def exchange(
    sections, tensors, cap,
    states, routes, lengths, gain_m, gain_a, weight_m, weight_a, heads_m, heads_a,
    scores, pairs, blocks, hidden,
    acc_m, acc_a, sq_m, sq_a, lanes, part, part_a, back, early, feats, outbox, inbox, work, wbuf_m, wbuf_a,
    dispatch, ended, picked,
    z_send, z_recv, m_send, m_recv, l_send, l_recv, b_send, b_recv, loc_sem, w_sem,
    t_send, t_recv, u_send, u_recv, r_send, r_recv, p_send, p_recv, g_send, g_recv, g_pass,
    h_send, h_recv, q_send, q_recv, y_send, y_recv,
):
    s = lax.axis_index("section")
    t = lax.axis_index("tensor")
    tok, fs = states.shape
    slots = sections * cap
    bw = blocks.shape[2]
    hid = acc_m.shape[1]
    nt = min(hid, 256)
    uw = fs // 2
    pieces = bw // uw
    half = tok // 2
    up_ok = t + 1 < tensors
    dn_ok = t > 0
    chips = sections // 2
    chip = s // 2
    core = lax.rem(s, 2)
    partner = s + 1 - 2 * core
    far = chips - 1 - chip
    near = slots - 2 * cap
    share = max(16, 5 * tok // 8 // tensors // 16 * 16)
    shared = share * tensors
    width = fs * tensors
    rb = 64

    def place(src, dest):
        return lax.rem(src // 2 + dest // 2, chips) * 2 + lax.rem(src, 2)

    def load(c):
        return pltpu.make_async_copy(states.at[:, pl.ds(c * uw, uw)], feats.at[2 * t + c], loc_sem.at[c])

    for c in range(2):
        load(c).start()

    barrier = pltpu.get_barrier_semaphore()

    def greet(r, c):
        pl.semaphore_signal(barrier, inc=1, device_id=(lax.rem(s + r, sections), t), device_id_type=MESH)
        return c

    lax.fori_loop(1, sections, greet, 0)

    def greet_z(r, c):
        pl.semaphore_signal(barrier, inc=1, device_id=(s, lax.rem(t + r, tensors)), device_id_type=MESH)
        return c

    lax.fori_loop(1, tensors, greet_z, 0)
    pl.semaphore_wait(barrier, sections - 1 + tensors - 1)
    for c in range(2):
        load(c).wait()

    parts = 2
    rows_z = tok // parts

    def z_copy(way, hop, c, h, shard, dest):
        rows = pl.ds(h * rows_z, rows_z)
        return pltpu.make_async_remote_copy(
            src_ref=feats.at[2 * shard + c, rows], dst_ref=feats.at[2 * shard + c, rows],
            send_sem=z_send.at[way, hop, c, h], recv_sem=z_recv.at[way, hop, c, h],
            device_id=(s, dest), device_id_type=MESH,
        )

    def m_copy(k, dest, src):
        return pltpu.make_async_remote_copy(
            src_ref=outbox.at[k, pl.ds(pl.multiple_of(dest * cap, cap), cap)],
            dst_ref=inbox.at[k, pl.ds(pl.multiple_of(place(src, dest) * cap, cap), cap)],
            send_sem=m_send.at[k, dest], recv_sem=m_recv.at[k, src],
            device_id=(dest, t), device_id_type=MESH,
        )

    def own_copy(k):
        return pltpu.make_async_copy(
            outbox.at[k, pl.ds(pl.multiple_of(s * cap, cap), cap)],
            inbox.at[k, pl.ds(pl.multiple_of(place(s, s) * cap, cap), cap)],
            m_recv.at[k, s],
        )

    def l_copy(way, hop, c, shard, dest):
        rows = pl.ds(near, 2 * cap)
        return pltpu.make_async_remote_copy(
            src_ref=inbox.at[2 * shard + c, rows], dst_ref=inbox.at[2 * shard + c, rows],
            send_sem=l_send.at[way, hop, c], recv_sem=l_recv.at[way, hop, c],
            device_id=(s, dest), device_id_type=MESH,
        )

    def b_dst(src, u, row, count):
        return blocks.at[src, pl.ds(row, count), pl.ds(pl.multiple_of(lax.rem(u, pieces) * uw, uw), uw)]

    def b_copy(u, src, first):
        dest = u // pieces
        piece = lax.rem(u, pieces)
        return pltpu.make_async_remote_copy(
            src_ref=feats.at[u, pl.ds(first, tok - first)], dst_ref=b_dst(src, u, first, tok - first),
            send_sem=b_send.at[dest, piece], recv_sem=b_recv.at[src, piece],
            device_id=(dest, t), device_id_type=MESH,
        )

    def own_block(u):
        return pltpu.make_async_copy(feats.at[u], b_dst(s, u, 0, tok), b_recv.at[s, lax.rem(u, pieces)])

    def q_copy(u, src):
        dest = u // pieces
        piece = lax.rem(u, pieces)
        row = pl.multiple_of(t * share, 16)
        return pltpu.make_async_remote_copy(
            src_ref=feats.at[u, pl.ds(row, share)], dst_ref=b_dst(src, u, row, share),
            send_sem=q_send.at[dest, piece], recv_sem=q_recv.at[src, piece],
            device_id=(dest, t), device_id_type=MESH,
        )

    def y_copy(way, hop, k, dest):
        rows = pl.ds(pl.multiple_of(k * share, 16), share)
        return pltpu.make_async_remote_copy(
            src_ref=blocks.at[pl.ds(far * 2, 2), rows], dst_ref=blocks.at[pl.ds(far * 2, 2), rows],
            send_sem=y_send.at[way, hop], recv_sem=y_recv.at[way, hop],
            device_id=(s, dest), device_id_type=MESH,
        )

    def w_copy(weight, buf, which, k):
        return pltpu.make_async_copy(
            weight.at[pl.ds(pl.multiple_of(k * uw, uw), uw)], buf, w_sem.at[which]
        )

    def line(way, hop):
        k = t - hop if way == 0 else t + hop
        here = k >= 0 if way == 0 else k < tensors
        onward = up_ok if way == 0 else dn_ok
        dest = t + 1 if way == 0 else t - 1
        return k, here, onward, dest

    def arrive(hop, c):
        for h in range(parts):
            for way in range(2):
                k, here, onward, dest = line(way, hop)

                @pl.when(jnp.logical_and(hop > 0, here))
                def _():
                    z_copy(way, hop, c, h, k, t).wait_recv()

                @pl.when(jnp.logical_and(here, onward))
                def _():
                    z_copy(way, hop + 1, c, h, k, dest).start()

    def slab_first(c):
        for j in range(2):
            m_copy(2 * t + c, s, far * 2 + j).wait_recv()
        for way in range(2):
            k, here, onward, dest = line(way, 0)

            @pl.when(onward)
            def _():
                l_copy(way, 1, c, t, dest).start()

    def slab_pass(hop, c):
        for way in range(2):
            k, here, onward, dest = line(way, hop)

            @pl.when(jnp.logical_and(here, onward))
            def _():
                l_copy(way, hop, c, k, t).wait_recv()
                l_copy(way, hop + 1, c, k, dest).start()

    def slab_end(hop, c):
        for way in range(2):
            k, here, onward, dest = line(way, hop)

            @pl.when(jnp.logical_and(here, jnp.logical_not(onward)))
            def _():
                l_copy(way, hop, c, k, t).wait_recv()

    def y_step(hop):
        for way in range(2):
            k, here, onward, dest = line(way, hop)

            @pl.when(jnp.logical_and(hop > 0, here))
            def _():
                y_copy(way, hop, k, t).wait_recv()

            @pl.when(jnp.logical_and(here, onward))
            def _():
                y_copy(way, hop + 1, k, dest).start()

    def both(hop, c, what):
        def inner(way, carry):
            k = jnp.where(way == 0, t - hop, t + hop)
            fine = jnp.logical_and(jnp.logical_and(k >= 0, k < tensors), jnp.logical_or(hop > 0, way == 0))

            @pl.when(fine)
            def _():
                what(2 * k + c)
            return carry

        lax.fori_loop(0, 2, inner, 0)

    def scale_rows(read, sq, first, gain, rows):
        def step(i, c):
            rr = pl.ds(pl.multiple_of(i * rb, rb), rb)
            x = read(pl.ds(pl.multiple_of(first + i * rb, rb), rb)).astype(jnp.float32)
            square = x * x
            total = square[:, 0:128]
            for j in range(1, uw // 128):
                total = total + square[:, j * 128:(j + 1) * 128]
            sq[pl.ds(pl.multiple_of(first + i * rb, rb), rb), :] += total
            work[rr, :] = (x * gain).astype(jnp.bfloat16)
            return c
        lax.fori_loop(0, rows // rb, step, 0)

    def accumulate(acc, first, rows, buf):
        def step(n, c):
            cols = pl.ds(pl.multiple_of(n * nt, nt), nt)
            acc[first:first + rows, cols] += jnp.dot(
                work[0:rows, :], buf[:, cols], preferred_element_type=jnp.float32
            )
            return c
        lax.fori_loop(0, hid // nt, step, 0)

    def pack(k):
        pt = min(uw, 256)

        def column(n, c):
            cols = pl.ds(pl.multiple_of(n * pt, pt), pt)
            outbox[k, :, cols] = jnp.dot(
                dispatch[...], feats[k, :, cols], preferred_element_type=jnp.float32
            ).astype(jnp.bfloat16)
            return c

        lax.fori_loop(0, uw // pt, column, 0)
        own_copy(k).start()

    def send(u, hop):
        @pl.when(hop == 0)
        def _():
            for j in range(2):
                m_copy(u, far * 2 + j, s).start()

        def one(r, c):
            dest = lax.rem(s + r, sections)

            @pl.when(dest // 2 != far)
            def _():
                m_copy(u, dest, s).start()
            return c

        lax.fori_loop(1, sections, one, 0)

    def send_block(u):
        dest = u // pieces

        @pl.when(dest == s)
        def _():
            own_block(u).start()

        @pl.when(jnp.logical_and(dest != s, dest // 2 != far))
        def _():
            b_copy(u, s, 0).start()

        @pl.when(dest // 2 == far)
        def _():
            q_copy(u, s).start()
            if shared < tok:
                b_copy(u, s, shared).start()

    def fetch(k):
        w_copy(weight_a, wbuf_a, 0, k).start()

    def actor(k):
        scale_rows(lambda rr: feats[k, rr, :], sq_a, 0, gain_a[k], tok)
        w_copy(weight_a, wbuf_a, 0, k).wait()
        accumulate(acc_a, 0, tok, wbuf_a)

    def member_near(k):
        w_copy(weight_m, wbuf_m, 1, k).start()
        own_copy(k).wait()

        def take(r, c):
            src = lax.rem(s + r, sections)

            @pl.when(src // 2 != far)
            def _():
                m_copy(k, s, src).wait_recv()
            return c

        lax.fori_loop(1, sections, take, 0)
        scale_rows(lambda rr: inbox[k, rr, :], sq_m, 0, gain_m[k], near)
        w_copy(weight_m, wbuf_m, 1, k).wait()
        accumulate(acc_m, 0, near, wbuf_m)

    def member_far(k):
        w_copy(weight_m, wbuf_m, 1, k).start()
        scale_rows(lambda rr: inbox[k, rr, :], sq_m, near, gain_m[k], slots - near)
        w_copy(weight_m, wbuf_m, 1, k).wait()
        accumulate(acc_m, near, slots - near, wbuf_m)

    def g_copy(dest, src):
        return pltpu.make_async_remote_copy(
            src_ref=early, dst_ref=hidden.at[src],
            send_sem=g_send.at[dest], recv_sem=g_recv.at[src],
            device_id=(dest, t), device_id_type=MESH,
        )

    def g_relay(src):
        return pltpu.make_async_remote_copy(
            src_ref=hidden.at[src], dst_ref=hidden.at[src],
            send_sem=g_pass.at[src], recv_sem=g_recv.at[src],
            device_id=(partner, t), device_id_type=MESH,
        )

    beside = (chip + 1 - 2 * lax.rem(chip, 2), chip + 2 - 4 * lax.rem(chip // 2, 2))

    def h_copy(i, src, dest):
        rows = pl.ds(i * half, half)
        return pltpu.make_async_remote_copy(
            src_ref=hidden.at[src, rows], dst_ref=hidden.at[src, rows],
            send_sem=h_send.at[i], recv_sem=h_recv.at[i],
            device_id=(dest, t), device_id_type=MESH,
        )

    def own_hidden():
        return pltpu.make_async_copy(early, hidden.at[s], g_recv.at[s])

    def t_copy(late, dest, src):
        spots = pl.ds(sections - 2, 2) if late else pl.ds(0, sections - 2)
        return pltpu.make_async_remote_copy(
            src_ref=part.at[src, spots], dst_ref=part.at[src, spots],
            send_sem=t_send.at[late, dest], recv_sem=t_recv.at[late, src],
            device_id=(s, dest), device_id_type=MESH,
        )

    def u_copy(dest, src):
        return pltpu.make_async_remote_copy(
            src_ref=part_a.at[src], dst_ref=part_a.at[src],
            send_sem=u_send.at[dest], recv_sem=u_recv.at[src],
            device_id=(s, dest), device_id_type=MESH,
        )

    def r_copy(dest, src):
        return pltpu.make_async_remote_copy(
            src_ref=scores.at[dest], dst_ref=back.at[src],
            send_sem=r_send.at[dest], recv_sem=r_recv.at[src],
            device_id=(dest, t), device_id_type=MESH,
        )

    def p_copy(dest, src):
        return pltpu.make_async_remote_copy(
            src_ref=pairs.at[src], dst_ref=pairs.at[src],
            send_sem=p_send.at[dest], recv_sem=p_recv.at[src],
            device_id=(dest, t), device_id_type=MESH,
        )

    def across(x):
        return lax.dot_general(
            jnp.ones((8, 128), jnp.float32), x, (((1,), (1,)), ((), ())),
            precision=lax.Precision.HIGHEST, preferred_element_type=jnp.float32,
        )

    def fold(x):
        total = x[:, 0:128]
        for j in range(1, hid // 128):
            total = total + x[:, j * 128:(j + 1) * 128]
        return total

    def prepare():
        target = jnp.broadcast_to(routes[...], (sections, tok))
        hit = target == lax.broadcasted_iota(jnp.int32, (sections, tok), 0)
        earlier = lax.broadcasted_iota(jnp.int32, (tok, tok), 0) < lax.broadcasted_iota(jnp.int32, (tok, tok), 1)
        placed = jnp.dot(
            hit.astype(jnp.float32).astype(jnp.bfloat16), earlier.astype(jnp.float32).astype(jnp.bfloat16),
            preferred_element_type=jnp.float32,
        )
        code = jnp.where(hit, placed, -1.0)
        slot = lax.broadcasted_iota(jnp.int32, (cap, tok), 0).astype(jnp.float32)
        for m in range(sections):
            here = slot == jnp.broadcast_to(code[m:m + 1, :], (cap, tok))
            dispatch[m * cap:(m + 1) * cap, :] = here.astype(jnp.float32).astype(jnp.bfloat16)

    def mark_ends():
        spot = lax.broadcasted_iota(jnp.int32, (8, tok), 1)
        end = lengths[0, 0]
        marks = (spot == end - 1).astype(jnp.float32)
        for i in range(1, lengths.shape[1]):
            end = end + lengths[0, i]
            marks = jnp.maximum(marks, (spot == end - 1).astype(jnp.float32))
        ended[...] = marks

    def hidden_step():
        def step(i, c):
            rr = pl.ds(pl.multiple_of(i * rb, rb), rb)
            scale = lax.rsqrt(jnp.sum(sq_a[rr, :], axis=1, keepdims=True) / width + epsilon)
            pre = acc_a[rr, :] * scale
            sig = 1.0 / (1.0 + jnp.exp(-pre))
            row = heads_a[...]
            early[rr, :] = (scale * row * (sig * (1.0 + pre * (1.0 - sig)))).astype(jnp.bfloat16)
            lanes[0, rr, :] = fold(pre * sig * row)
            return c

        lax.fori_loop(0, tok // rb, step, 0)
        own_hidden().start()
        g_copy(partner, s).start()

        def send_g(r, c):
            oc = lax.rem(chip + r, chips)

            @pl.when(oc != far)
            def _():
                g_copy(oc * 2 + core, s).start()
            return c

        lax.fori_loop(1, chips, send_g, 0)
        part_a[t] = across(lanes[0, 0:tok, :])

        def send_u(r, c):
            u_copy(lax.rem(t + r, tensors), t).start()
            return c

        lax.fori_loop(1, tensors, send_u, 0)

    def hand_on():
        def relay(r, c):
            oc = lax.rem(chip + r, chips)

            @pl.when(oc != far)
            def _():
                g_copy(s, oc * 2 + core).wait_recv()
                for i in range(2):
                    @pl.when(oc == chips - 1 - beside[i])
                    def _():
                        h_copy(i, oc * 2 + core, beside[i] * 2 + core).start()
                g_relay(oc * 2 + core).start()
            return c

        lax.fori_loop(1, chips, relay, 0)
        own_hidden().wait()

    def hand_far():
        for i in range(2):
            h_copy(i, far * 2 + core, s).wait_recv()
        g_relay(far * 2 + core).start()

    def score_rows(first, rows):
        def step(i, c):
            rr = pl.ds(pl.multiple_of(first + i * rb, rb), rb)
            scale = lax.rsqrt(jnp.sum(sq_m[rr, :], axis=1, keepdims=True) / width + epsilon)
            pre = acc_m[rr, :] * scale
            act = pre * (1.0 / (1.0 + jnp.exp(-pre)))
            lanes[0, rr, :] = fold(act * heads_m[0:1, :])
            lanes[1, rr, :] = fold(act * heads_m[1:2, :])
            return c

        lax.fori_loop(0, rows // rb, step, 0)

    def send_part(late):
        first, rows = (near, slots - near) if late else (0, near)
        top = lax.broadcasted_iota(jnp.int32, (8, rows), 0) == 0
        both_rows = jnp.where(
            top, across(lanes[0, first:first + rows, :]), across(lanes[1, first:first + rows, :])
        )
        for p in range(rows // cap):
            part[t, first // cap + p] = both_rows[:, p * cap:(p + 1) * cap]

        def send_t(r, c):
            t_copy(late, lax.rem(t + r, tensors), t).start()
            return c

        lax.fori_loop(1, tensors, send_t, 0)

    def take_part(late):
        def take_t(r, c):
            t_copy(late, t, lax.rem(t + r, tensors)).wait_recv()
            return c

        lax.fori_loop(1, tensors, take_t, 0)

    def give_back(d):
        spot = place(d, s)
        scores[d] = lax.fori_loop(1, tensors, lambda k, v: v + part[k, spot], part[0, spot])

    def pick(m):
        x = back[m]
        hi = x.astype(jnp.bfloat16)
        rest = x - hi.astype(jnp.float32)
        mid = rest.astype(jnp.bfloat16)
        low = (rest - mid.astype(jnp.float32)).astype(jnp.bfloat16)
        rows = dispatch[pl.ds(pl.multiple_of(m * cap, cap), cap), :]
        v = picked[...]
        for piece in (low, mid, hi):
            v = v + jnp.dot(piece, rows, preferred_element_type=jnp.float32)
        picked[...] = v

    def give_near():
        take_part(0)
        give_back(s)
        back[s] = scores[s]

        def one(r, c):
            d = lax.rem(s + r, sections)

            @pl.when(d // 2 != far)
            def _():
                give_back(d)
                r_copy(d, s).start()
            return c

        lax.fori_loop(1, sections, one, 0)

        def take_u(r, c):
            u_copy(t, lax.rem(t + r, tensors)).wait_recv()
            return c

        lax.fori_loop(1, tensors, take_u, 0)

    def pick_near():
        picked[...] = jnp.zeros_like(picked)
        pick(s)

        def one(r, c):
            m = lax.rem(s + r, sections)

            @pl.when(m // 2 != far)
            def _():
                r_copy(s, m).wait_recv()
                pick(m)
            return c

        lax.fori_loop(1, sections, one, 0)

    def score_step():
        send_part(1)
        y_step(tensors - 2)
        pick_near()
        shift = lax.fori_loop(1, tensors, lambda k, v: v + part_a[k], part_a[0])
        take_part(1)
        for j in range(2):
            give_back(far * 2 + j)
            r_copy(far * 2 + j, s).start()
        for j in range(2):
            r_copy(s, far * 2 + j).wait_recv()
            pick(far * 2 + j)

        values = jnp.broadcast_to(picked[0:1, :], (8, tok))
        rewards = jnp.broadcast_to(picked[1:2, :], (8, tok))
        stop = ended[...] > 0.5
        total = jnp.where(stop, rewards, pltpu.roll(values, tok - 1, 1)) - values
        carry = jnp.where(stop, 0.0, trace_decay)
        step = 1
        while step < tok:
            total = total + carry * pltpu.roll(total, tok - step, 1)
            carry = carry * pltpu.roll(carry, tok - step, 1)
            step *= 2
        first = lax.broadcasted_iota(jnp.int32, (8, tok), 0) == 0
        pairs[s] = jnp.where(first, total, shift)

        def send_p(r, c):
            p_copy(lax.rem(s + r, sections), s).start()
            return c

        lax.fori_loop(1, sections, send_p, 0)

    arrive(0, 0)
    prepare()

    def ship(u, hop):
        pack(u)
        send(u, hop)
        send_block(u)

    def turn_of(j):
        return lax.rem(j, tensors), j // tensors

    fetch(2 * t)
    ship(2 * t, 0)
    ship(2 * t + 1, 0)
    acc_m[...] = jnp.zeros_like(acc_m)
    acc_a[...] = jnp.zeros_like(acc_a)
    sq_m[...] = jnp.zeros_like(sq_m)
    sq_a[...] = jnp.zeros_like(sq_a)
    mark_ends()
    actor(2 * t)
    lag = 6

    def turn(j, carry):
        hop, c = turn_of(j)
        arrive(hop, c)

        @pl.when(j >= 2 * tensors - 2)
        def _():
            slab_first(j - (2 * tensors - 2))

        def take(u):
            fetch(u)

            @pl.when(hop > 0)
            def _():
                ship(u, hop)

            actor(u)

        both(hop, c, take)

        @pl.when(j >= lag)
        def _():
            both(*turn_of(j - lag), member_near)
        return carry

    lax.fori_loop(1, 2 * tensors, turn, 0)
    hidden_step()

    def passes(j, carry):
        slab_pass(j // 2, lax.rem(j, 2))
        return carry

    lax.fori_loop(2, 4, passes, 0)

    def rest(j, carry):
        both(*turn_of(j), member_near)
        return carry

    cut = 2 * tensors - 3
    lax.fori_loop(2 * tensors - lag, cut, rest, 0)
    lax.fori_loop(4, 2 * tensors - 2, passes, 0)
    lax.fori_loop(cut, 2 * tensors, rest, 0)
    score_rows(0, near)
    send_part(0)

    def far_rows(j, carry):
        hop, c = j // 2, lax.rem(j, 2)

        @pl.when(hop > 0)
        def _():
            slab_end(hop, c)

        both(hop, c, member_far)

        @pl.when(j == 3)
        def _():
            def shares(p, carry):
                for i in range(2):
                    q_copy(s * pieces + p, far * 2 + i).wait_recv()
                return carry

            lax.fori_loop(0, pieces, shares, 0)
            y_step(0)
            hand_on()

        @pl.when(jnp.logical_and(jnp.logical_and(hop > 1, c == 1), hop < tensors - 1))
        def _():
            y_step(hop - 1)

        @pl.when(j == 5)
        def _():
            give_near()
        return carry

    lax.fori_loop(0, 2 * tensors, far_rows, 0)
    score_rows(near, slots - near)
    score_step()
    hand_far()

    g_copy(s, partner).wait_recv()
    g_copy(partner, s).wait_send()

    def done_g(r, c):
        oc = lax.rem(chip + r, chips)

        @pl.when(oc != far)
        def _():
            g_copy(oc * 2 + core, s).wait_send()

        g_relay(oc * 2 + core).wait_send()
        g_copy(s, oc * 2 + 1 - core).wait_recv()
        return c

    lax.fori_loop(1, chips, done_g, 0)
    for i in range(2):
        h_copy(i, (chips - 1 - beside[i]) * 2 + core, beside[i] * 2 + core).wait_send()

    def done_z(r, c):
        other = lax.rem(t + r, tensors)
        t_copy(0, other, t).wait_send()
        t_copy(1, other, t).wait_send()
        u_copy(other, t).wait_send()
        return c

    lax.fori_loop(1, tensors, done_z, 0)
    y_step(tensors - 1)

    def done_b(p, carry):
        own_block(s * pieces + p).wait()
        for i in range(2):
            q_copy((far * 2 + i) * pieces + p, s).wait_send()

        def one(r, carry):
            other = lax.rem(s + r, sections)

            @pl.when(other // 2 != far)
            def _():
                b_copy(s * pieces + p, other, 0).wait_recv()
                b_copy(other * pieces + p, s, 0).wait_send()

            if shared < tok:
                @pl.when(other // 2 == far)
                def _():
                    b_copy(s * pieces + p, other, shared).wait_recv()
                    b_copy(other * pieces + p, s, shared).wait_send()
            return carry

        return lax.fori_loop(1, sections, one, carry)

    lax.fori_loop(0, pieces, done_b, 0)

    def done_s(r, c):
        other = lax.rem(s + r, sections)
        r_copy(other, s).wait_send()
        p_copy(other, s).wait_send()
        p_copy(s, other).wait_recv()

        def sent(u, c):
            @pl.when(jnp.logical_or(other // 2 != far, u // 2 == t))
            def _():
                m_copy(u, other, s).wait_send()
            return c

        return lax.fori_loop(0, 2 * tensors, sent, c)

    lax.fori_loop(1, sections, done_s, 0)

    def drain(hop, carry):
        for way in range(2):
            k, here, onward, dest = line(way, hop)

            @pl.when(jnp.logical_and(here, onward))
            def _():
                y_copy(way, hop + 1, k, dest).wait_send()
                for c in range(2):
                    for h in range(parts):
                        z_copy(way, hop + 1, c, h, k, dest).wait_send()
                    l_copy(way, hop + 1, c, k, dest).wait_send()
        return carry

    lax.fori_loop(0, tensors, drain, 0)


def gradient(pairs, scores, gain, blocks, hidden, packed, norm, grad, raw, slope):
    sections, _, tok = pairs.shape
    cap = scores.shape[2]
    s = lax.axis_index("section")
    i = pl.program_id(0)

    @pl.when(i == 0)
    def _():
        for j in range(sections):
            raw[0, j:j + 1, :] = pairs[j, 0:1, :]
            raw[1, j:j + 1, :] = pairs[j, 1:2, :]
            packed[:, j * cap:(j + 1) * cap] = scores[j, 0:2, :]
        total = sections * tok
        value = raw[0]
        center = jnp.sum(jnp.sum(value, axis=1, keepdims=True), axis=0, keepdims=True) / total
        square = jnp.sum(jnp.sum(value * value, axis=1, keepdims=True), axis=0, keepdims=True) / total
        inv = lax.rsqrt(square - center * center + epsilon)
        ratios = jnp.exp(raw[1])
        slope[...] = penalty * (ratios - 1.0) - ratios * ((value - center) * inv)
        norm[...] = (pairs[s][0:1, :] - center) * inv

    per, _, wide = hidden.shape
    last = sections // per - 1
    def scaled(p):
        column = jnp.transpose(jnp.broadcast_to(slope[pl.ds(i * per + p, 1), :], (128, tok)))
        return jnp.concatenate(
            [
                (hidden[p, :, j * 128:(j + 1) * 128].astype(jnp.float32) * column).astype(jnp.bfloat16)
                for j in range(wide // 128)
            ],
            axis=1,
        )

    right = jnp.concatenate([scaled(p) for p in range(per)], axis=0)
    left = blocks[...].reshape(per * tok, blocks.shape[2])
    product = lax.dot_general(left, right, (((0,), (0,)), ((), ())), preferred_element_type=jnp.float32)

    @pl.when(i == 0)
    def _():
        grad[...] = product

    @pl.when(jnp.logical_and(i > 0, i < last))
    def _():
        grad[...] += product

    @pl.when(i == last)
    def _():
        rows = product.shape[0]
        own = jnp.transpose(jnp.broadcast_to(gain[s], (128, rows)))
        for j in range(wide // 128):
            cols = slice(j * 128, (j + 1) * 128)
            grad[:, cols] = (grad[:, cols] + product[:, cols]) * own


def body(
    states, lengths, routes, score_gain, score_weight, score_heads,
    actor_gain, actor_weight, actor_heads,
):
    sections = lax.axis_size("section")
    tensors = lax.axis_size("tensor")
    tok, fs = states.shape
    cap = 2 * tok // sections
    slots = sections * cap
    width = score_gain.shape[1]
    hid = actor_weight.shape[1]
    bw = width // sections
    uw = fs // 2
    pieces = bw // uw

    vmem = pl.BlockSpec(memory_space=pltpu.VMEM)
    smem = pl.BlockSpec(memory_space=pltpu.SMEM)
    any_ = pl.BlockSpec(memory_space=pl.ANY)
    f32, bf16 = jnp.float32, jnp.bfloat16
    dma = pltpu.SemaphoreType.DMA
    scores, pairs, blocks, hidden = pl.pallas_call(
        functools.partial(exchange, sections, tensors, cap),
        out_shape=(
            jax.ShapeDtypeStruct((sections, 8, cap), f32),
            jax.ShapeDtypeStruct((sections, 8, tok), f32),
            jax.ShapeDtypeStruct((sections, tok, bw), bf16),
            jax.ShapeDtypeStruct((sections, tok, hid), bf16),
        ),
        in_specs=[any_, vmem, smem, vmem, vmem, any_, any_, vmem, vmem],
        out_specs=(vmem, vmem, any_, any_),
        scratch_shapes=[
            pltpu.VMEM((slots, hid), f32),
            pltpu.VMEM((tok, hid), f32),
            pltpu.VMEM((slots, 128), f32),
            pltpu.VMEM((tok, 128), f32),
            pltpu.VMEM((2, max(slots, tok), 128), f32),
            pltpu.VMEM((tensors, sections, 8, cap), f32),
            pltpu.VMEM((tensors, 8, tok), f32),
            pltpu.VMEM((sections, 8, cap), f32),
            pltpu.VMEM((tok, hid), bf16),
            pltpu.VMEM((2 * tensors, tok, uw), bf16),
            pltpu.VMEM((2 * tensors, slots, uw), bf16),
            pltpu.VMEM((2 * tensors, slots, uw), bf16),
            pltpu.VMEM((max(tok, slots - 2 * cap), uw), bf16),
            pltpu.VMEM((uw, hid), bf16),
            pltpu.VMEM((uw, hid), bf16),
            pltpu.VMEM((slots, tok), bf16),
            pltpu.VMEM((8, tok), f32),
            pltpu.VMEM((8, tok), f32),
            dma((2, tensors + 1, 2, 2)),
            dma((2, tensors + 1, 2, 2)),
            dma((2 * tensors, sections)),
            dma((2 * tensors, sections)),
            dma((2, tensors + 1, 2)),
            dma((2, tensors + 1, 2)),
            dma((sections, pieces)),
            dma((sections, pieces)),
            dma((2,)),
            dma((2,)),
            dma((2, tensors)),
            dma((2, tensors)),
            dma((tensors,)),
            dma((tensors,)),
            dma((sections,)),
            dma((sections,)),
            dma((sections,)),
            dma((sections,)),
            dma((sections,)),
            dma((sections,)),
            dma((sections,)),
            dma((2,)),
            dma((2,)),
            dma((sections, pieces)),
            dma((sections, pieces)),
            dma((2, tensors + 1)),
            dma((2, tensors + 1)),
        ],
        compiler_params=pltpu.CompilerParams(
            collective_id=0, has_side_effects=True, vmem_limit_bytes=67043328
        ),
    )(
        states, routes.reshape(1, tok), lengths, score_gain[0].reshape(2 * tensors, 1, uw),
        actor_gain.reshape(2 * tensors, 1, uw), score_weight[0], actor_weight,
        jnp.transpose(score_heads[0]), actor_heads[None, :],
    )

    packed_scores, norm, actor_grad = pl.pallas_call(
        gradient,
        grid=(sections // 2,),
        out_shape=(
            jax.ShapeDtypeStruct((2, slots), f32),
            jax.ShapeDtypeStruct((1, tok), f32),
            jax.ShapeDtypeStruct((bw, hid), f32),
        ),
        in_specs=[
            pl.BlockSpec((sections, 8, tok), lambda i: (0, 0, 0)),
            pl.BlockSpec((sections, 8, cap), lambda i: (0, 0, 0)),
            pl.BlockSpec((sections, 1, bw), lambda i: (0, 0, 0)),
            pl.BlockSpec((2, tok, bw), lambda i: (i, 0, 0)),
            pl.BlockSpec((2, tok, hid), lambda i: (i, 0, 0)),
        ],
        out_specs=(
            pl.BlockSpec((2, slots), lambda i: (0, 0)),
            pl.BlockSpec((1, tok), lambda i: (0, 0)),
            pl.BlockSpec((bw, hid), lambda i: (0, 0)),
        ),
        scratch_shapes=[pltpu.VMEM((2, sections, tok), f32), pltpu.VMEM((sections, tok), f32)],
        compiler_params=pltpu.CompilerParams(vmem_limit_bytes=50 * 1024 * 1024),
    )(pairs, scores, actor_gain.reshape(sections, 1, bw), blocks, hidden)
    return (packed_scores, norm[0], actor_grad)


def solution(mesh):
    in_specs = (
        P("section", "tensor"),
        P("section", None),
        P("section", None),
        P("section", None),
        P("section", None, "tensor"),
        P("section", "tensor", None),
        P(),
        P(None, "tensor"),
        P("tensor"),
    )
    out_specs = (P(None, "section"), P("section"), P("section", "tensor"))
    return jax.shard_map(body, mesh=mesh, in_specs=in_specs, out_specs=out_specs, check_vma=False)
```

```python
import functools
import jax
import jax.numpy as jnp
from jax import lax
from jax.experimental import pallas as pl
from jax.experimental.pallas import tpu as pltpu
from jax.sharding import PartitionSpec as P

epsilon = 1e-05
trace_decay = 0.95
penalty = 0.1
MESH = pl.DeviceIdType.MESH


def exchange(
    sections, tensors, cap,
    states, routes, lengths, gain_m, gain_a, weight_m, weight_a, heads_m, heads_a,
    scores, pairs, blocks, hidden,
    acc_m, acc_a, sq_m, sq_a, lanes, part, part_a, back, early, feats, outbox, inbox, work, wbuf_m, wbuf_a,
    dispatch, ended, picked,
    z_send, z_recv, m_send, m_recv, l_send, l_recv, b_send, b_recv, loc_sem, w_sem,
    t_send, t_recv, u_send, u_recv, r_send, r_recv, p_send, p_recv, g_send, g_recv, g_pass,
    h_send, h_recv, q_send, q_recv, y_send, y_recv,
):
    s = lax.axis_index("section")
    t = lax.axis_index("tensor")
    tok, fs = states.shape
    slots = sections * cap
    bw = blocks.shape[2]
    hid = acc_m.shape[1]
    nt = min(hid, 256)
    uw = fs // 2
    pieces = bw // uw
    half = tok // 2
    up_ok = t + 1 < tensors
    dn_ok = t > 0
    chips = sections // 2
    chip = s // 2
    core = lax.rem(s, 2)
    partner = s + 1 - 2 * core
    far = chips - 1 - chip
    near = slots - 2 * cap
    share = max(16, 5 * tok // 8 // tensors // 16 * 16)
    shared = share * tensors
    width = fs * tensors
    rb = 64

    def place(src, dest):
        return lax.rem(src // 2 + dest // 2, chips) * 2 + lax.rem(src, 2)

    def load(c):
        return pltpu.make_async_copy(states.at[:, pl.ds(c * uw, uw)], feats.at[2 * t + c], loc_sem.at[c])

    for c in range(2):
        load(c).start()

    barrier = pltpu.get_barrier_semaphore()

    def greet(r, c):
        pl.semaphore_signal(barrier, inc=1, device_id=(lax.rem(s + r, sections), t), device_id_type=MESH)
        return c

    lax.fori_loop(1, sections, greet, 0)

    def greet_z(r, c):
        pl.semaphore_signal(barrier, inc=1, device_id=(s, lax.rem(t + r, tensors)), device_id_type=MESH)
        return c

    lax.fori_loop(1, tensors, greet_z, 0)
    pl.semaphore_wait(barrier, sections - 1 + tensors - 1)
    for c in range(2):
        load(c).wait()

    parts = 2
    rows_z = tok // parts

    def z_copy(way, hop, c, h, shard, dest):
        rows = pl.ds(h * rows_z, rows_z)
        return pltpu.make_async_remote_copy(
            src_ref=feats.at[2 * shard + c, rows], dst_ref=feats.at[2 * shard + c, rows],
            send_sem=z_send.at[way, hop, c, h], recv_sem=z_recv.at[way, hop, c, h],
            device_id=(s, dest), device_id_type=MESH,
        )

    def m_copy(k, dest, src):
        return pltpu.make_async_remote_copy(
            src_ref=outbox.at[k, pl.ds(pl.multiple_of(dest * cap, cap), cap)],
            dst_ref=inbox.at[k, pl.ds(pl.multiple_of(place(src, dest) * cap, cap), cap)],
            send_sem=m_send.at[k, dest], recv_sem=m_recv.at[k, src],
            device_id=(dest, t), device_id_type=MESH,
        )

    def own_copy(k):
        return pltpu.make_async_copy(
            outbox.at[k, pl.ds(pl.multiple_of(s * cap, cap), cap)],
            inbox.at[k, pl.ds(pl.multiple_of(place(s, s) * cap, cap), cap)],
            m_recv.at[k, s],
        )

    def l_copy(way, hop, c, shard, dest):
        rows = pl.ds(near, 2 * cap)
        return pltpu.make_async_remote_copy(
            src_ref=inbox.at[2 * shard + c, rows], dst_ref=inbox.at[2 * shard + c, rows],
            send_sem=l_send.at[way, hop, c], recv_sem=l_recv.at[way, hop, c],
            device_id=(s, dest), device_id_type=MESH,
        )

    def b_dst(src, u, row, count):
        return blocks.at[src, pl.ds(row, count), pl.ds(pl.multiple_of(lax.rem(u, pieces) * uw, uw), uw)]

    def b_copy(u, src, first):
        dest = u // pieces
        piece = lax.rem(u, pieces)
        return pltpu.make_async_remote_copy(
            src_ref=feats.at[u, pl.ds(first, tok - first)], dst_ref=b_dst(src, u, first, tok - first),
            send_sem=b_send.at[dest, piece], recv_sem=b_recv.at[src, piece],
            device_id=(dest, t), device_id_type=MESH,
        )

    def own_block(u):
        return pltpu.make_async_copy(feats.at[u], b_dst(s, u, 0, tok), b_recv.at[s, lax.rem(u, pieces)])

    def q_copy(u, src):
        dest = u // pieces
        piece = lax.rem(u, pieces)
        row = pl.multiple_of(t * share, 16)
        return pltpu.make_async_remote_copy(
            src_ref=feats.at[u, pl.ds(row, share)], dst_ref=b_dst(src, u, row, share),
            send_sem=q_send.at[dest, piece], recv_sem=q_recv.at[src, piece],
            device_id=(dest, t), device_id_type=MESH,
        )

    def y_copy(way, hop, k, dest):
        rows = pl.ds(pl.multiple_of(k * share, 16), share)
        return pltpu.make_async_remote_copy(
            src_ref=blocks.at[pl.ds(far * 2, 2), rows], dst_ref=blocks.at[pl.ds(far * 2, 2), rows],
            send_sem=y_send.at[way, hop], recv_sem=y_recv.at[way, hop],
            device_id=(s, dest), device_id_type=MESH,
        )

    def w_copy(weight, buf, which, k):
        return pltpu.make_async_copy(
            weight.at[pl.ds(pl.multiple_of(k * uw, uw), uw)], buf, w_sem.at[which]
        )

    def line(way, hop):
        k = t - hop if way == 0 else t + hop
        here = k >= 0 if way == 0 else k < tensors
        onward = up_ok if way == 0 else dn_ok
        dest = t + 1 if way == 0 else t - 1
        return k, here, onward, dest

    def arrive(hop, c):
        for h in range(parts):
            for way in range(2):
                k, here, onward, dest = line(way, hop)

                @pl.when(jnp.logical_and(hop > 0, here))
                def _():
                    z_copy(way, hop, c, h, k, t).wait_recv()

                @pl.when(jnp.logical_and(here, onward))
                def _():
                    z_copy(way, hop + 1, c, h, k, dest).start()

    def slab_first(c):
        for j in range(2):
            m_copy(2 * t + c, s, far * 2 + j).wait_recv()
        for way in range(2):
            k, here, onward, dest = line(way, 0)

            @pl.when(onward)
            def _():
                l_copy(way, 1, c, t, dest).start()

    def slab_pass(hop, c):
        for way in range(2):
            k, here, onward, dest = line(way, hop)

            @pl.when(jnp.logical_and(here, onward))
            def _():
                l_copy(way, hop, c, k, t).wait_recv()
                l_copy(way, hop + 1, c, k, dest).start()

    def slab_end(hop, c):
        for way in range(2):
            k, here, onward, dest = line(way, hop)

            @pl.when(jnp.logical_and(here, jnp.logical_not(onward)))
            def _():
                l_copy(way, hop, c, k, t).wait_recv()

    def y_step(hop):
        for way in range(2):
            k, here, onward, dest = line(way, hop)

            @pl.when(jnp.logical_and(hop > 0, here))
            def _():
                y_copy(way, hop, k, t).wait_recv()

            @pl.when(jnp.logical_and(here, onward))
            def _():
                y_copy(way, hop + 1, k, dest).start()

    def both(hop, c, what):
        def inner(way, carry):
            k = jnp.where(way == 0, t - hop, t + hop)
            fine = jnp.logical_and(jnp.logical_and(k >= 0, k < tensors), jnp.logical_or(hop > 0, way == 0))

            @pl.when(fine)
            def _():
                what(2 * k + c)
            return carry

        lax.fori_loop(0, 2, inner, 0)

    def scale_rows(read, sq, first, gain, rows):
        def step(i, c):
            rr = pl.ds(pl.multiple_of(i * rb, rb), rb)
            x = read(pl.ds(pl.multiple_of(first + i * rb, rb), rb)).astype(jnp.float32)
            square = x * x
            total = square[:, 0:128]
            for j in range(1, uw // 128):
                total = total + square[:, j * 128:(j + 1) * 128]
            sq[pl.ds(pl.multiple_of(first + i * rb, rb), rb), :] += total
            work[rr, :] = (x * gain).astype(jnp.bfloat16)
            return c
        lax.fori_loop(0, rows // rb, step, 0)

    def accumulate(acc, first, rows, buf):
        def step(n, c):
            cols = pl.ds(pl.multiple_of(n * nt, nt), nt)
            acc[first:first + rows, cols] += jnp.dot(
                work[0:rows, :], buf[:, cols], preferred_element_type=jnp.float32
            )
            return c
        lax.fori_loop(0, hid // nt, step, 0)

    def pack(k):
        pt = min(uw, 256)

        def column(n, c):
            cols = pl.ds(pl.multiple_of(n * pt, pt), pt)
            outbox[k, :, cols] = jnp.dot(
                dispatch[...], feats[k, :, cols], preferred_element_type=jnp.float32
            ).astype(jnp.bfloat16)
            return c

        lax.fori_loop(0, uw // pt, column, 0)
        own_copy(k).start()

    def send(u, hop):
        @pl.when(hop == 0)
        def _():
            for j in range(2):
                m_copy(u, far * 2 + j, s).start()

        def one(r, c):
            dest = lax.rem(s + r, sections)

            @pl.when(dest // 2 != far)
            def _():
                m_copy(u, dest, s).start()
            return c

        lax.fori_loop(1, sections, one, 0)

    def send_block(u):
        dest = u // pieces

        @pl.when(dest == s)
        def _():
            own_block(u).start()

        @pl.when(jnp.logical_and(dest != s, dest // 2 != far))
        def _():
            b_copy(u, s, 0).start()

        @pl.when(dest // 2 == far)
        def _():
            q_copy(u, s).start()
            if shared < tok:
                b_copy(u, s, shared).start()

    def fetch(k):
        w_copy(weight_a, wbuf_a, 0, k).start()

    def actor(k):
        scale_rows(lambda rr: feats[k, rr, :], sq_a, 0, gain_a[k], tok)
        w_copy(weight_a, wbuf_a, 0, k).wait()
        accumulate(acc_a, 0, tok, wbuf_a)

    def member_near(k):
        w_copy(weight_m, wbuf_m, 1, k).start()
        own_copy(k).wait()

        def take(r, c):
            src = lax.rem(s + r, sections)

            @pl.when(src // 2 != far)
            def _():
                m_copy(k, s, src).wait_recv()
            return c

        lax.fori_loop(1, sections, take, 0)
        scale_rows(lambda rr: inbox[k, rr, :], sq_m, 0, gain_m[k], near)
        w_copy(weight_m, wbuf_m, 1, k).wait()
        accumulate(acc_m, 0, near, wbuf_m)

    def member_far(k):
        w_copy(weight_m, wbuf_m, 1, k).start()
        scale_rows(lambda rr: inbox[k, rr, :], sq_m, near, gain_m[k], slots - near)
        w_copy(weight_m, wbuf_m, 1, k).wait()
        accumulate(acc_m, near, slots - near, wbuf_m)

    def g_copy(dest, src):
        return pltpu.make_async_remote_copy(
            src_ref=early, dst_ref=hidden.at[src],
            send_sem=g_send.at[dest], recv_sem=g_recv.at[src],
            device_id=(dest, t), device_id_type=MESH,
        )

    def g_relay(src):
        return pltpu.make_async_remote_copy(
            src_ref=hidden.at[src], dst_ref=hidden.at[src],
            send_sem=g_pass.at[src], recv_sem=g_recv.at[src],
            device_id=(partner, t), device_id_type=MESH,
        )

    beside = (chip + 1 - 2 * lax.rem(chip, 2), chip + 2 - 4 * lax.rem(chip // 2, 2))

    def h_copy(i, src, dest):
        rows = pl.ds(i * half, half)
        return pltpu.make_async_remote_copy(
            src_ref=hidden.at[src, rows], dst_ref=hidden.at[src, rows],
            send_sem=h_send.at[i], recv_sem=h_recv.at[i],
            device_id=(dest, t), device_id_type=MESH,
        )

    def own_hidden():
        return pltpu.make_async_copy(early, hidden.at[s], g_recv.at[s])

    def t_copy(late, dest, src):
        spots = pl.ds(sections - 2, 2) if late else pl.ds(0, sections - 2)
        return pltpu.make_async_remote_copy(
            src_ref=part.at[src, spots], dst_ref=part.at[src, spots],
            send_sem=t_send.at[late, dest], recv_sem=t_recv.at[late, src],
            device_id=(s, dest), device_id_type=MESH,
        )

    def u_copy(dest, src):
        return pltpu.make_async_remote_copy(
            src_ref=part_a.at[src], dst_ref=part_a.at[src],
            send_sem=u_send.at[dest], recv_sem=u_recv.at[src],
            device_id=(s, dest), device_id_type=MESH,
        )

    def r_copy(dest, src):
        return pltpu.make_async_remote_copy(
            src_ref=scores.at[dest], dst_ref=back.at[src],
            send_sem=r_send.at[dest], recv_sem=r_recv.at[src],
            device_id=(dest, t), device_id_type=MESH,
        )

    def p_copy(dest, src):
        return pltpu.make_async_remote_copy(
            src_ref=pairs.at[src], dst_ref=pairs.at[src],
            send_sem=p_send.at[dest], recv_sem=p_recv.at[src],
            device_id=(dest, t), device_id_type=MESH,
        )

    def across(x):
        return lax.dot_general(
            jnp.ones((8, 128), jnp.float32), x, (((1,), (1,)), ((), ())),
            precision=lax.Precision.HIGHEST, preferred_element_type=jnp.float32,
        )

    def fold(x):
        total = x[:, 0:128]
        for j in range(1, hid // 128):
            total = total + x[:, j * 128:(j + 1) * 128]
        return total

    def prepare():
        target = jnp.broadcast_to(routes[...], (sections, tok))
        hit = target == lax.broadcasted_iota(jnp.int32, (sections, tok), 0)
        earlier = lax.broadcasted_iota(jnp.int32, (tok, tok), 0) < lax.broadcasted_iota(jnp.int32, (tok, tok), 1)
        placed = jnp.dot(
            hit.astype(jnp.float32).astype(jnp.bfloat16), earlier.astype(jnp.float32).astype(jnp.bfloat16),
            preferred_element_type=jnp.float32,
        )
        code = jnp.where(hit, placed, -1.0)
        slot = lax.broadcasted_iota(jnp.int32, (cap, tok), 0).astype(jnp.float32)
        for m in range(sections):
            here = slot == jnp.broadcast_to(code[m:m + 1, :], (cap, tok))
            dispatch[m * cap:(m + 1) * cap, :] = here.astype(jnp.float32).astype(jnp.bfloat16)

    def mark_ends():
        spot = lax.broadcasted_iota(jnp.int32, (8, tok), 1)
        end = lengths[0, 0]
        marks = (spot == end - 1).astype(jnp.float32)
        for i in range(1, lengths.shape[1]):
            end = end + lengths[0, i]
            marks = jnp.maximum(marks, (spot == end - 1).astype(jnp.float32))
        ended[...] = marks

    def hidden_step():
        def step(i, c):
            rr = pl.ds(pl.multiple_of(i * rb, rb), rb)
            scale = lax.rsqrt(jnp.sum(sq_a[rr, :], axis=1, keepdims=True) / width + epsilon)
            pre = acc_a[rr, :] * scale
            sig = 1.0 / (1.0 + jnp.exp(-pre))
            row = heads_a[...]
            early[rr, :] = (scale * row * (sig * (1.0 + pre * (1.0 - sig)))).astype(jnp.bfloat16)
            lanes[0, rr, :] = fold(pre * sig * row)
            return c

        lax.fori_loop(0, tok // rb, step, 0)
        own_hidden().start()
        g_copy(partner, s).start()

        def send_g(r, c):
            oc = lax.rem(chip + r, chips)

            @pl.when(oc != far)
            def _():
                g_copy(oc * 2 + core, s).start()
            return c

        lax.fori_loop(1, chips, send_g, 0)
        part_a[t] = across(lanes[0, 0:tok, :])

        def send_u(r, c):
            u_copy(lax.rem(t + r, tensors), t).start()
            return c

        lax.fori_loop(1, tensors, send_u, 0)

    def hand_on():
        def relay(r, c):
            oc = lax.rem(chip + r, chips)

            @pl.when(oc != far)
            def _():
                g_copy(s, oc * 2 + core).wait_recv()
                for i in range(2):
                    @pl.when(oc == chips - 1 - beside[i])
                    def _():
                        h_copy(i, oc * 2 + core, beside[i] * 2 + core).start()
                g_relay(oc * 2 + core).start()
            return c

        lax.fori_loop(1, chips, relay, 0)
        own_hidden().wait()

    def hand_far():
        for i in range(2):
            h_copy(i, far * 2 + core, s).wait_recv()
        g_relay(far * 2 + core).start()

    def score_rows(first, rows):
        def step(i, c):
            rr = pl.ds(pl.multiple_of(first + i * rb, rb), rb)
            scale = lax.rsqrt(jnp.sum(sq_m[rr, :], axis=1, keepdims=True) / width + epsilon)
            pre = acc_m[rr, :] * scale
            act = pre * (1.0 / (1.0 + jnp.exp(-pre)))
            lanes[0, rr, :] = fold(act * heads_m[0:1, :])
            lanes[1, rr, :] = fold(act * heads_m[1:2, :])
            return c

        lax.fori_loop(0, rows // rb, step, 0)

    def send_part(late):
        first, rows = (near, slots - near) if late else (0, near)
        top = lax.broadcasted_iota(jnp.int32, (8, rows), 0) == 0
        both_rows = jnp.where(
            top, across(lanes[0, first:first + rows, :]), across(lanes[1, first:first + rows, :])
        )
        for p in range(rows // cap):
            part[t, first // cap + p] = both_rows[:, p * cap:(p + 1) * cap]

        def send_t(r, c):
            t_copy(late, lax.rem(t + r, tensors), t).start()
            return c

        lax.fori_loop(1, tensors, send_t, 0)

    def take_part(late):
        def take_t(r, c):
            t_copy(late, t, lax.rem(t + r, tensors)).wait_recv()
            return c

        lax.fori_loop(1, tensors, take_t, 0)

    def give_back(d):
        spot = place(d, s)
        scores[d] = lax.fori_loop(1, tensors, lambda k, v: v + part[k, spot], part[0, spot])

    def pick(m):
        x = back[m]
        hi = x.astype(jnp.bfloat16)
        rest = x - hi.astype(jnp.float32)
        mid = rest.astype(jnp.bfloat16)
        low = (rest - mid.astype(jnp.float32)).astype(jnp.bfloat16)
        rows = dispatch[pl.ds(pl.multiple_of(m * cap, cap), cap), :]
        v = picked[...]
        for piece in (low, mid, hi):
            v = v + jnp.dot(piece, rows, preferred_element_type=jnp.float32)
        picked[...] = v

    def give_near():
        take_part(0)
        give_back(s)
        back[s] = scores[s]

        def one(r, c):
            d = lax.rem(s + r, sections)

            @pl.when(d // 2 != far)
            def _():
                give_back(d)
                r_copy(d, s).start()
            return c

        lax.fori_loop(1, sections, one, 0)

        def take_u(r, c):
            u_copy(t, lax.rem(t + r, tensors)).wait_recv()
            return c

        lax.fori_loop(1, tensors, take_u, 0)

    def pick_near():
        picked[...] = jnp.zeros_like(picked)
        pick(s)

        def one(r, c):
            m = lax.rem(s + r, sections)

            @pl.when(m // 2 != far)
            def _():
                r_copy(s, m).wait_recv()
                pick(m)
            return c

        lax.fori_loop(1, sections, one, 0)

    def score_step():
        send_part(1)
        y_step(tensors - 2)
        pick_near()
        shift = lax.fori_loop(1, tensors, lambda k, v: v + part_a[k], part_a[0])
        take_part(1)
        for j in range(2):
            give_back(far * 2 + j)
            r_copy(far * 2 + j, s).start()
        for j in range(2):
            r_copy(s, far * 2 + j).wait_recv()
            pick(far * 2 + j)

        values = jnp.broadcast_to(picked[0:1, :], (8, tok))
        rewards = jnp.broadcast_to(picked[1:2, :], (8, tok))
        stop = ended[...] > 0.5
        total = jnp.where(stop, rewards, pltpu.roll(values, tok - 1, 1)) - values
        carry = jnp.where(stop, 0.0, trace_decay)
        step = 1
        while step < tok:
            total = total + carry * pltpu.roll(total, tok - step, 1)
            carry = carry * pltpu.roll(carry, tok - step, 1)
            step *= 2
        first = lax.broadcasted_iota(jnp.int32, (8, tok), 0) == 0
        pairs[s] = jnp.where(first, total, shift)

        def send_p(r, c):
            p_copy(lax.rem(s + r, sections), s).start()
            return c

        lax.fori_loop(1, sections, send_p, 0)

    arrive(0, 0)
    prepare()

    def ship(u, hop):
        pack(u)
        send(u, hop)
        send_block(u)

    def turn_of(j):
        return lax.rem(j, tensors), j // tensors

    fetch(2 * t)
    ship(2 * t, 0)
    ship(2 * t + 1, 0)
    acc_m[...] = jnp.zeros_like(acc_m)
    acc_a[...] = jnp.zeros_like(acc_a)
    sq_m[...] = jnp.zeros_like(sq_m)
    sq_a[...] = jnp.zeros_like(sq_a)
    mark_ends()
    actor(2 * t)
    lag = 6

    def turn(j, carry):
        hop, c = turn_of(j)
        arrive(hop, c)

        @pl.when(j >= 2 * tensors - 2)
        def _():
            slab_first(j - (2 * tensors - 2))

        def take(u):
            fetch(u)

            @pl.when(hop > 0)
            def _():
                ship(u, hop)

            actor(u)

        both(hop, c, take)

        @pl.when(j >= lag)
        def _():
            both(*turn_of(j - lag), member_near)
        return carry

    lax.fori_loop(1, 2 * tensors, turn, 0)
    hidden_step()

    def passes(j, carry):
        slab_pass(j // 2, lax.rem(j, 2))
        return carry

    lax.fori_loop(2, 4, passes, 0)

    def rest(j, carry):
        both(*turn_of(j), member_near)
        return carry

    cut = 2 * tensors - 3
    lax.fori_loop(2 * tensors - lag, cut, rest, 0)
    lax.fori_loop(4, 2 * tensors - 2, passes, 0)
    lax.fori_loop(cut, 2 * tensors, rest, 0)
    score_rows(0, near)
    send_part(0)

    def far_rows(j, carry):
        hop, c = j // 2, lax.rem(j, 2)

        @pl.when(hop > 0)
        def _():
            slab_end(hop, c)

        both(hop, c, member_far)

        @pl.when(j == 3)
        def _():
            def shares(p, carry):
                for i in range(2):
                    q_copy(s * pieces + p, far * 2 + i).wait_recv()
                return carry

            lax.fori_loop(0, pieces, shares, 0)
            y_step(0)
            hand_on()

        @pl.when(jnp.logical_and(jnp.logical_and(hop > 1, c == 1), hop < tensors - 1))
        def _():
            y_step(hop - 1)

        @pl.when(j == 5)
        def _():
            give_near()
        return carry

    lax.fori_loop(0, 2 * tensors, far_rows, 0)
    score_rows(near, slots - near)
    score_step()
    hand_far()

    g_copy(s, partner).wait_recv()
    g_copy(partner, s).wait_send()

    def done_g(r, c):
        oc = lax.rem(chip + r, chips)

        @pl.when(oc != far)
        def _():
            g_copy(oc * 2 + core, s).wait_send()

        g_relay(oc * 2 + core).wait_send()
        g_copy(s, oc * 2 + 1 - core).wait_recv()
        return c

    lax.fori_loop(1, chips, done_g, 0)
    for i in range(2):
        h_copy(i, (chips - 1 - beside[i]) * 2 + core, beside[i] * 2 + core).wait_send()

    def done_z(r, c):
        other = lax.rem(t + r, tensors)
        t_copy(0, other, t).wait_send()
        t_copy(1, other, t).wait_send()
        u_copy(other, t).wait_send()
        return c

    lax.fori_loop(1, tensors, done_z, 0)
    y_step(tensors - 1)

    def done_b(p, carry):
        own_block(s * pieces + p).wait()
        for i in range(2):
            q_copy((far * 2 + i) * pieces + p, s).wait_send()

        def one(r, carry):
            other = lax.rem(s + r, sections)

            @pl.when(other // 2 != far)
            def _():
                b_copy(s * pieces + p, other, 0).wait_recv()
                b_copy(other * pieces + p, s, 0).wait_send()

            if shared < tok:
                @pl.when(other // 2 == far)
                def _():
                    b_copy(s * pieces + p, other, shared).wait_recv()
                    b_copy(other * pieces + p, s, shared).wait_send()
            return carry

        return lax.fori_loop(1, sections, one, carry)

    lax.fori_loop(0, pieces, done_b, 0)

    def done_s(r, c):
        other = lax.rem(s + r, sections)
        r_copy(other, s).wait_send()
        p_copy(other, s).wait_send()
        p_copy(s, other).wait_recv()

        def sent(u, c):
            @pl.when(jnp.logical_or(other // 2 != far, u // 2 == t))
            def _():
                m_copy(u, other, s).wait_send()
            return c

        return lax.fori_loop(0, 2 * tensors, sent, c)

    lax.fori_loop(1, sections, done_s, 0)

    def drain(hop, carry):
        for way in range(2):
            k, here, onward, dest = line(way, hop)

            @pl.when(jnp.logical_and(here, onward))
            def _():
                y_copy(way, hop + 1, k, dest).wait_send()
                for c in range(2):
                    for h in range(parts):
                        z_copy(way, hop + 1, c, h, k, dest).wait_send()
                    l_copy(way, hop + 1, c, k, dest).wait_send()
        return carry

    lax.fori_loop(0, tensors, drain, 0)


def gradient(pairs, scores, gain, blocks, hidden, packed, norm, grad, raw, slope):
    sections, _, tok = pairs.shape
    cap = scores.shape[2]
    s = lax.axis_index("section")
    i = pl.program_id(0)

    @pl.when(i == 0)
    def _():
        for j in range(sections):
            raw[0, j:j + 1, :] = pairs[j, 0:1, :]
            raw[1, j:j + 1, :] = pairs[j, 1:2, :]
            packed[:, j * cap:(j + 1) * cap] = scores[j, 0:2, :]
        total = sections * tok
        value = raw[0]
        center = jnp.sum(jnp.sum(value, axis=1, keepdims=True), axis=0, keepdims=True) / total
        square = jnp.sum(jnp.sum(value * value, axis=1, keepdims=True), axis=0, keepdims=True) / total
        inv = lax.rsqrt(square - center * center + epsilon)
        ratios = jnp.exp(raw[1])
        slope[...] = penalty * (ratios - 1.0) - ratios * ((value - center) * inv)
        norm[...] = (pairs[s][0:1, :] - center) * inv

    per, _, wide = hidden.shape
    last = sections // per - 1
    def scaled(p):
        column = jnp.transpose(jnp.broadcast_to(slope[pl.ds(i * per + p, 1), :], (128, tok)))
        return jnp.concatenate(
            [
                (hidden[p, :, j * 128:(j + 1) * 128].astype(jnp.float32) * column).astype(jnp.bfloat16)
                for j in range(wide // 128)
            ],
            axis=1,
        )

    right = jnp.concatenate([scaled(p) for p in range(per)], axis=0)
    left = blocks[...].reshape(per * tok, blocks.shape[2])
    product = lax.dot_general(left, right, (((0,), (0,)), ((), ())), preferred_element_type=jnp.float32)

    @pl.when(i == 0)
    def _():
        grad[...] = product

    @pl.when(jnp.logical_and(i > 0, i < last))
    def _():
        grad[...] += product

    @pl.when(i == last)
    def _():
        rows = product.shape[0]
        own = jnp.transpose(jnp.broadcast_to(gain[s], (128, rows)))
        for j in range(wide // 128):
            cols = slice(j * 128, (j + 1) * 128)
            grad[:, cols] = (grad[:, cols] + product[:, cols]) * own


def body(
    states, lengths, routes, score_gain, score_weight, score_heads,
    actor_gain, actor_weight, actor_heads,
):
    sections = lax.axis_size("section")
    tensors = lax.axis_size("tensor")
    tok, fs = states.shape
    cap = 2 * tok // sections
    slots = sections * cap
    width = score_gain.shape[1]
    hid = actor_weight.shape[1]
    bw = width // sections
    uw = fs // 2
    pieces = bw // uw

    vmem = pl.BlockSpec(memory_space=pltpu.VMEM)
    smem = pl.BlockSpec(memory_space=pltpu.SMEM)
    any_ = pl.BlockSpec(memory_space=pl.ANY)
    f32, bf16 = jnp.float32, jnp.bfloat16
    dma = pltpu.SemaphoreType.DMA
    scores, pairs, blocks, hidden = pl.pallas_call(
        functools.partial(exchange, sections, tensors, cap),
        out_shape=(
            jax.ShapeDtypeStruct((sections, 8, cap), f32),
            jax.ShapeDtypeStruct((sections, 8, tok), f32),
            jax.ShapeDtypeStruct((sections, tok, bw), bf16),
            jax.ShapeDtypeStruct((sections, tok, hid), bf16),
        ),
        in_specs=[any_, vmem, smem, vmem, vmem, any_, any_, vmem, vmem],
        out_specs=(vmem, vmem, any_, any_),
        scratch_shapes=[
            pltpu.VMEM((slots, hid), f32),
            pltpu.VMEM((tok, hid), f32),
            pltpu.VMEM((slots, 128), f32),
            pltpu.VMEM((tok, 128), f32),
            pltpu.VMEM((2, max(slots, tok), 128), f32),
            pltpu.VMEM((tensors, sections, 8, cap), f32),
            pltpu.VMEM((tensors, 8, tok), f32),
            pltpu.VMEM((sections, 8, cap), f32),
            pltpu.VMEM((tok, hid), bf16),
            pltpu.VMEM((2 * tensors, tok, uw), bf16),
            pltpu.VMEM((2 * tensors, slots, uw), bf16),
            pltpu.VMEM((2 * tensors, slots, uw), bf16),
            pltpu.VMEM((max(tok, slots - 2 * cap), uw), bf16),
            pltpu.VMEM((uw, hid), bf16),
            pltpu.VMEM((uw, hid), bf16),
            pltpu.VMEM((slots, tok), bf16),
            pltpu.VMEM((8, tok), f32),
            pltpu.VMEM((8, tok), f32),
            dma((2, tensors + 1, 2, 2)),
            dma((2, tensors + 1, 2, 2)),
            dma((2 * tensors, sections)),
            dma((2 * tensors, sections)),
            dma((2, tensors + 1, 2)),
            dma((2, tensors + 1, 2)),
            dma((sections, pieces)),
            dma((sections, pieces)),
            dma((2,)),
            dma((2,)),
            dma((2, tensors)),
            dma((2, tensors)),
            dma((tensors,)),
            dma((tensors,)),
            dma((sections,)),
            dma((sections,)),
            dma((sections,)),
            dma((sections,)),
            dma((sections,)),
            dma((sections,)),
            dma((sections,)),
            dma((2,)),
            dma((2,)),
            dma((sections, pieces)),
            dma((sections, pieces)),
            dma((2, tensors + 1)),
            dma((2, tensors + 1)),
        ],
        compiler_params=pltpu.CompilerParams(
            collective_id=0, has_side_effects=True, vmem_limit_bytes=67043328
        ),
    )(
        states, routes.reshape(1, tok), lengths, score_gain[0].reshape(2 * tensors, 1, uw),
        actor_gain.reshape(2 * tensors, 1, uw), score_weight[0], actor_weight,
        jnp.transpose(score_heads[0]), actor_heads[None, :],
    )

    packed_scores, norm, actor_grad = pl.pallas_call(
        gradient,
        grid=(sections // 2,),
        out_shape=(
            jax.ShapeDtypeStruct((2, slots), f32),
            jax.ShapeDtypeStruct((1, tok), f32),
            jax.ShapeDtypeStruct((bw, hid), f32),
        ),
        in_specs=[
            pl.BlockSpec((sections, 8, tok), lambda i: (0, 0, 0)),
            pl.BlockSpec((sections, 8, cap), lambda i: (0, 0, 0)),
            pl.BlockSpec((sections, 1, bw), lambda i: (0, 0, 0)),
            pl.BlockSpec((2, tok, bw), lambda i: (i, 0, 0)),
            pl.BlockSpec((2, tok, hid), lambda i: (i, 0, 0)),
        ],
        out_specs=(
            pl.BlockSpec((2, slots), lambda i: (0, 0)),
            pl.BlockSpec((1, tok), lambda i: (0, 0)),
            pl.BlockSpec((bw, hid), lambda i: (0, 0)),
        ),
        scratch_shapes=[pltpu.VMEM((2, sections, tok), f32), pltpu.VMEM((sections, tok), f32)],
        compiler_params=pltpu.CompilerParams(vmem_limit_bytes=67043328),
    )(pairs, scores, actor_gain.reshape(sections, 1, bw), blocks, hidden)
    return (packed_scores, norm[0], actor_grad)


def solution(mesh):
    in_specs = (
        P("section", "tensor"),
        P("section", None),
        P("section", None),
        P("section", None),
        P("section", None, "tensor"),
        P("section", "tensor", None),
        P(),
        P(None, "tensor"),
        P("tensor"),
    )
    out_specs = (P(None, "section"), P("section"), P("section", "tensor"))
    return jax.shard_map(body, mesh=mesh, in_specs=in_specs, out_specs=out_specs, check_vma=False)
```
